256 devices in a mesh: chan: 4 (over z_hi), rows: 64 (over x, z_lo, y, core).
Axes of the slice: x: 4, y: 4, z: 8 (z_hi: 4, z_lo: 2; z = z_hi * 2 + z_lo), core: 2. Of those that a mesh axis runs over, the one named last changes fastest.
Arguments:
- tokens: bfloat16 [512, 512, 512], P('rows', None, 'chan'), may hold values from -60 to 60
- gain_in: float32 [512], P('chan'), may hold values from 0.1 to 1.9
- spectral_w1: float32 [2, 8, 64, 64], P(None, 'chan'), may hold values from -0.75 to 0.75
- spectral_b1: float32 [2, 8, 64], P(None, 'chan'), may hold values from -3 to 3
- spectral_w2: float32 [2, 8, 64, 64], P(None, 'chan'), may hold values from -0.75 to 0.75
- spectral_b2: float32 [2, 8, 64], P(None, 'chan'), may hold values from -3 to 3
- gain_out: float32 [512], replicated, may hold values from 0.1 to 1.9
- fc1_weight: bfloat16 [512, 2048], P(None, 'chan'), may hold values from -0.25 to 0.25
- fc1_bias: bfloat16 [2048], P('chan'), may hold values from -3 to 3
- fc2_weight: bfloat16 [2048, 512], P('chan'), may hold values from -0.1875 to 0.1875
- fc2_bias: bfloat16 [512], P('chan'), may hold values from -3 to 3
Outputs:
- block_out: bfloat16 [512, 512, 512], P('rows', None, 'chan')
The draws below stay inside these ranges and needn't reach their ends.
All inputs are finite; a program needn't handle non-finite values.
Results may differ from the reference program's by a relative error of at most 0.0055.
Values may be sent and summed in bfloat16 or wider, within the bound.
No kernel may reach another device: no remote copies, remote signals or barrier semaphores. Data moves between devices by JAX's collectives and lax.ppermute only.
A program may use at most 64 MiB of HBM per device.

```python
from functools import partial
import jax
import jax.numpy as jnp
from jax import lax

HEIGHT = 512
WIDTH = 512
DIM = 512
BLOCKS = 8
FFN = 2048
BLOCK = 64


def draw_tokens(key, part):
    key_base, key_chan, key_token, key_shift = jax.random.split(key, 4)
    ramp = 3.0 ** (jnp.arange(DIM, dtype=jnp.float32) / DIM)
    chan_scale = jnp.exp(jax.random.uniform(key_chan, (DIM,), jnp.float32, jnp.log(0.3), 0.0)) * ramp
    token_scale = jnp.exp(jax.random.uniform(key_token, (HEIGHT, WIDTH, 1), jnp.float32, 0.0, jnp.log(3.0)))
    base = jax.random.normal(key_base, (HEIGHT, WIDTH, DIM), jnp.float32)
    shift = 0.5 * jax.random.normal(key_shift, (DIM,), jnp.float32)
    base = jnp.clip(base, -5.0, 5.0)
    shift = jnp.clip(shift, -3.0, 3.0)
    return ((base * token_scale + shift) * chan_scale).astype(jnp.bfloat16)


def raised(values, rng, source, target, blocks, factor):
    def block_of(dim):
        return (jnp.arange(values.shape[dim]) // (values.shape[dim] // blocks)).reshape((-1,) + (1,) * (values.ndim - 1 - dim))

    one_side = jax.random.permutation(rng, blocks)[block_of(target)]
    other_side = (block_of(target) + blocks // 2) % blocks
    return jnp.where((block_of(source) == one_side) | (block_of(source) == other_side), factor * values, values)


def block_scale(own_key, extent, shards, smallest, high):
    level = 1.0
    for position, shards_of in shards:
        draws = jax.random.uniform(jax.random.fold_in(jax.random.fold_in(own_key, 6), position), (shards_of,), jnp.float32, smallest / len(shards), high / len(shards))
        level = level * jnp.repeat(jnp.exp(draws), extent[position] // shards_of).reshape((-1,) + (1,) * (len(extent) - 1 - position))
    return level


def bell_draw(own_key, extent, scale, limit, pieces=(), kind=jnp.bfloat16):
    values = scale * jax.random.normal(own_key, extent, jnp.float32)
    if pieces:
        values = values * block_scale(own_key, extent, pieces, -0.22, 0.18)
    return jnp.clip(values, -limit, limit).astype(kind)


def noise_with(key, shape, scale, limit, shards, heavy, kind=jnp.bfloat16):
    drawn = scale * jax.random.normal(key, shape, jnp.float32)
    if shards:
        drawn = drawn * block_scale(key, shape, shards, -0.22, 0.18)
    return jnp.clip(raised(drawn, jax.random.fold_in(key, 3), *heavy), -limit, limit).astype(kind)


def setup_inputs(seed: int = 0) -> dict:
    splits = jax.random.split(jax.random.key(seed), 12)
    return {
        "tokens": draw_tokens(jax.random.fold_in(splits[11], 71), 0),
        "gain_in": jnp.clip(1.0 + 0.18 * jax.random.normal(splits[1], (DIM,), jnp.float32), 0.1, 1.9),
        "spectral_w1": bell_draw(splits[2], (2, BLOCKS, BLOCK, BLOCK), BLOCK ** -0.5, 0.75, ((1, 4),), jnp.float32),
        "spectral_b1": bell_draw(splits[3], (2, BLOCKS, BLOCK), 0.5, 3.0, ((1, 4),), jnp.float32),
        "spectral_w2": bell_draw(splits[4], (2, BLOCKS, BLOCK, BLOCK), BLOCK ** -0.5, 0.75, ((1, 4),), jnp.float32),
        "spectral_b2": bell_draw(splits[5], (2, BLOCKS, BLOCK), 0.5, 3.0, ((1, 4),), jnp.float32),
        "gain_out": jnp.clip(1.0 + 0.18 * jax.random.normal(splits[6], (DIM,), jnp.float32), 0.1, 1.9),
        "fc1_weight": bell_draw(splits[7], (DIM, FFN), DIM ** -0.5, 0.25, ((1, 4),)),
        "fc1_bias": bell_draw(splits[8], (FFN,), 0.5, 3.0, ((0, 4),)),
        "fc2_weight": noise_with(splits[9], (FFN, DIM), FFN ** -0.5, 0.1875, ((0, 4),), (0, 1, 4, 2.0)),
        "fc2_bias": bell_draw(splits[10], (DIM,), 0.5, 3.0, ((0, 4),)),
    }


norm_eps = 1e-05
shrink_level = 0.01
highest = lax.Precision.HIGHEST

def normalize(values, gain):
    center = lax.optimization_barrier(jnp.mean(values, axis=-1, keepdims=True))
    spread = lax.optimization_barrier(jnp.mean(values * values, axis=-1, keepdims=True)) - center * center
    return (values - center) * lax.rsqrt(spread + norm_eps) * gain

def soften(values):
    return jnp.where(values > shrink_level, values - shrink_level, jnp.where(values < -shrink_level, values + shrink_level, 0.0))

def block_layer(real_part, imag_part, weights, biases):
    product = partial(jnp.einsum, 'hknb,nbo->hkno', precision=highest)
    weights = weights.astype(jnp.float32)
    return (product(real_part, weights[0]) - product(imag_part, weights[1]) + biases[0], product(imag_part, weights[0]) + product(real_part, weights[1]) + biases[1])

def feed_forward(token_block, gain_out, fc1_weight, fc1_bias, fc2_weight, fc2_bias):
    source = token_block.astype(jnp.float32)
    normed = normalize(source, gain_out).astype(jnp.bfloat16)
    hidden = jax.nn.gelu(jnp.dot(normed, fc1_weight, preferred_element_type=jnp.float32) + fc1_bias.astype(jnp.float32), approximate=False).astype(jnp.bfloat16)
    summed = jnp.dot(hidden, fc2_weight, preferred_element_type=jnp.float32)
    return (source + summed + fc2_bias.astype(jnp.float32)).astype(jnp.bfloat16)

def reference(tokens, gain_in, spectral_w1, spectral_b1, spectral_w2, spectral_b2, gain_out, fc1_weight, fc1_bias, fc2_weight, fc2_bias):
    source = tokens.astype(jnp.float32)
    normed = normalize(source, gain_in)
    spectrum = jnp.fft.rfft2(normed, axes=(0, 1), norm='ortho')[:, :WIDTH // 2, :]
    real_part = jnp.real(spectrum).astype(jnp.float32).reshape(HEIGHT, WIDTH // 2, BLOCKS, BLOCK)
    imag_part = jnp.imag(spectrum).astype(jnp.float32).reshape(HEIGHT, WIDTH // 2, BLOCKS, BLOCK)
    first_real, first_imag = block_layer(real_part, imag_part, spectral_w1, spectral_b1)
    first_real = jnp.maximum(first_real, 0.0)
    first_imag = jnp.maximum(first_imag, 0.0)
    second_real, second_imag = block_layer(first_real, first_imag, spectral_w2, spectral_b2)
    shrunk_real = soften(second_real).reshape(HEIGHT, WIDTH // 2, DIM)
    shrunk_imag = soften(second_imag).reshape(HEIGHT, WIDTH // 2, DIM)
    combined = lax.complex(shrunk_real, shrunk_imag)
    combined = jnp.pad(combined, ((0, 0), (0, 1), (0, 0)))
    filtered = jnp.fft.irfft2(combined, s=(HEIGHT, WIDTH), axes=(0, 1), norm='ortho').astype(jnp.float32)
    mixed = (filtered + normed + source).astype(jnp.bfloat16)
    blocks = mixed.reshape(64, -1, DIM)

    def one_block(token_block):
        return feed_forward(token_block, gain_out, fc1_weight, fc1_bias, fc2_weight, fc2_bias)
    result = lax.map(one_block, blocks)
    return result.reshape(HEIGHT, WIDTH, DIM)
```

```python
import math
from functools import partial

import jax
import jax.numpy as jnp
import numpy as np
from jax import lax
from jax.experimental import pallas as pl
from jax.experimental.pallas import tpu as pltpu
from jax.sharding import PartitionSpec as P

norm_eps = 1e-05
shrink_level = 0.01
bf16 = jnp.bfloat16
f32 = jnp.float32


def tables(rows, width, per_owner):
    owners = width // 2 // per_owner
    place = np.arange(width)
    freq = np.arange(width // 2).reshape(owners, 1, per_owner)
    freq = np.broadcast_to(freq, (owners, 2, per_owner)).reshape(-1)
    part = np.broadcast_to(np.arange(2).reshape(1, 2, 1), (owners, 2, per_owner)).reshape(-1)
    angle = 2.0 * np.pi / width * ((freq[:, None] * place[None, :]) % width)
    forward = np.where(part[:, None] == 0, np.cos(angle), -np.sin(angle))
    inverse = (forward * np.where(freq == 0, 1.0, 2.0)[:, None]).T
    grid = np.arange(rows)
    turn = 2.0 * np.pi / rows * ((grid[:, None] * grid[None, :]) % rows)
    return forward, inverse, np.cos(turn), np.sin(turn)


def mm(left, right):
    return jnp.dot(left, right, preferred_element_type=f32)


def mm_t(left, right):
    return lax.dot_general(left, right, (((1,), (1,)), ((), ())), preferred_element_type=f32)


def stats_kernel(x_ref, bias_ref, o_ref):
    rows, width, lanes = x_ref.shape
    o_ref[2] = jnp.zeros((rows, width), f32)
    o_ref[2, 0:1, 0:lanes] = bias_ref[...]
    ones = jnp.ones((8, x_ref.shape[2]), bf16)
    for row in range(rows):
        x = x_ref[row]
        wide = x.astype(f32)
        square = wide * wide
        high = square.astype(bf16)
        low = (square - high.astype(f32)).astype(bf16)
        o_ref[0, row : row + 1, :] = mm_t(ones, x)[0:1]
        o_ref[1, row : row + 1, :] = (mm_t(ones, high) + mm_t(ones, low))[0:1]


def forward_kernel(channels, scale, x_ref, s0_ref, s1_ref, s2_ref, s3_ref, gain_ref, table_ref, o_ref, r_ref):
    rows, width, lanes = x_ref.shape
    owners = o_ref.shape[0]
    total = (s0_ref[0] + s1_ref[0]) + (s2_ref[0] + s3_ref[0])
    square = (s0_ref[1] + s1_ref[1]) + (s2_ref[1] + s3_ref[1])
    center = total / channels
    spread = square / channels - center * center
    flipped = jnp.transpose(jnp.concatenate([center, lax.rsqrt(spread + norm_eps)], axis=0))
    gain = gain_ref[...]
    for pair in range(rows // 2):
        sides = []
        for row in (2 * pair, 2 * pair + 1):
            x = x_ref[row].astype(f32)
            normed = (x - flipped[:, row : row + 1]) * flipped[:, rows + row : rows + row + 1] * gain
            r_ref[row] = normed + x
            sides.append(normed.astype(bf16))
        out = mm(table_ref[...], jnp.concatenate(sides, axis=1)) * scale
        for side in range(2):
            o_ref[:, 2 * pair + side] = (
                out[:, side * lanes : (side + 1) * lanes].reshape(owners, -1, lanes).astype(bf16)
            )


def soften(values):
    return jnp.where(
        values > shrink_level,
        values - shrink_level,
        jnp.where(values < -shrink_level, values + shrink_level, 0.0),
    )


def column_kernel(
    scale, x_ref, cos_ref, sin_ref, w1_ref, b1_ref, w2_ref, b2_ref, o_ref, wide_ref, real_ref, imag_ref
):
    height = cos_ref.shape[0]
    lanes = x_ref.shape[1]
    step = x_ref.shape[0] // height
    count = step // 2
    wide_ref[...] = x_ref[...].astype(f32)
    for part, target in ((0, real_ref), (1, imag_ref)):
        for k in range(count):
            target[:, k * lanes : (k + 1) * lanes] = wide_ref[
                pl.ds(part * count + k, height, stride=step), :
            ].astype(bf16)
    for half in range(count // 2):
        span = pl.ds(half * 2 * lanes, 2 * lanes)
        cos, sin = cos_ref[...], sin_ref[...]
        real, imag = real_ref[:, span], imag_ref[:, span]
        out_real = (mm(cos, real) + mm(sin, imag)) * scale
        out_imag = (mm(cos, imag) - mm(sin, real)) * scale
        next_real, next_imag = [], []
        for side in range(2):
            cut = slice(side * lanes, (side + 1) * lanes)
            both = jnp.concatenate([out_real[:, cut].astype(bf16), out_imag[:, cut].astype(bf16)], axis=1)
            first = jnp.maximum(mm(both, w1_ref[...]) + b1_ref[...], 0.0).astype(bf16)
            second = soften(mm(first, w2_ref[...]) + b2_ref[...]).astype(bf16)
            next_real.append(second[:, :lanes])
            next_imag.append(second[:, lanes:])
        real, imag = jnp.concatenate(next_real, axis=1), jnp.concatenate(next_imag, axis=1)
        back_real = (mm(cos, real) - mm(sin, imag)) * scale
        back_imag = (mm(cos, imag) + mm(sin, real)) * scale
        for side in range(2):
            cut = slice(side * lanes, (side + 1) * lanes)
            k = half * 2 + side
            wide_ref[pl.ds(k, height, stride=step), :] = back_real[:, cut]
            wide_ref[pl.ds(count + k, height, stride=step), :] = back_imag[:, cut]
    o_ref[...] = wide_ref[...].astype(bf16)


def inverse_kernel(scale, me_ref, x_ref, table_ref, r_ref, *o_refs):
    ways = len(o_refs)
    rows, width, lanes = r_ref.shape
    group = rows // ways
    me = me_ref[0]
    for shift in range(ways):
        owner = lax.rem(me + shift, ways)
        for pair in range(group // 2):
            first = owner * group + 2 * pair
            sides = [
                x_ref[:, first + side].astype(f32).reshape(-1, lanes).astype(bf16) for side in range(2)
            ]
            out = mm(table_ref[...], jnp.concatenate(sides, axis=1)) * scale
            for side in range(2):
                o_refs[shift][pl.ds((2 * pair + side) * width, width), :] = (
                    out[:, side * lanes : (side + 1) * lanes] + r_ref[first + side]
                ).astype(bf16)


def gelu(values):
    return 0.5 * values * (1.0 + lax.erf(values * math.sqrt(0.5)))


def mlp_kernel(tile, me_ref, x0, x1, x2, x3, wa_ref, wb_ref, gain_ref, s0, s1, s2, s3, y0, y1, y2, y3, x_ref, y_ref, b_ref):
    ways, tokens, lanes = x_ref.shape
    channels = ways * lanes
    me = me_ref[0]
    biases_out = (s0, s1, s2, s3)
    for shift, ref in enumerate((x0, x1, x2, x3)):
        x_ref[lax.rem(me + ways - shift, ways)] = ref[...]
        b_ref[pl.ds(lax.rem(me + ways - shift, ways), 1), :] = biases_out[shift][2, 0:1, 0:lanes]
    unit = jnp.ones((8, lanes), bf16)
    hidden_block = 512
    biases = []
    for ref in (wa_ref, wb_ref):
        for start in range(0, ref.shape[0], hidden_block):
            biases.append(mm_t(unit, ref[start : start + hidden_block, 2 * channels :])[0:1])

    def body(index, carry):
        span = pl.ds(pl.multiple_of(index * tile, tile), tile)
        mixed = [x_ref[block, span, :].astype(f32) for block in range(ways)]
        total = sum(mixed[1:], mixed[0])
        square = sum((m * m for m in mixed[1:]), mixed[0] * mixed[0])
        center = jnp.sum(total, axis=1, keepdims=True) / channels
        spread = jnp.sum(square, axis=1, keepdims=True) / channels - center * center
        inverse = lax.rsqrt(spread + norm_eps)
        normed = jnp.concatenate(
            [
                ((m - center) * inverse * gain_ref[:, b * lanes : (b + 1) * lanes]).astype(bf16)
                for b, m in enumerate(mixed)
            ],
            axis=1,
        )
        acc = None
        block = 0
        for ref in (wa_ref, wb_ref):
            for start in range(0, ref.shape[0], hidden_block):
                rows = pl.ds(start, hidden_block)
                hidden = gelu(mm_t(normed, ref[rows, :channels]) + biases[block]).astype(bf16)
                product = mm(hidden, ref[rows, channels : 2 * channels])
                acc = product if acc is None else acc + product
                block += 1
        for b in range(ways):
            cut = slice(b * lanes, (b + 1) * lanes)
            y_ref[b, span, :] = (mixed[b] + acc[:, cut] + b_ref[b : b + 1, :]).astype(bf16)
        return carry

    lax.fori_loop(0, tokens // tile, body, 0)
    for shift, ref in enumerate((y0, y1, y2, y3)):
        ref[...] = y_ref[lax.rem(me + shift, ways)]


def vmem(count):
    return [pl.BlockSpec(memory_space=pltpu.VMEM)] * count


smem = pl.BlockSpec(memory_space=pltpu.SMEM)


def call(kernel, shapes, in_specs, scratch=(), flops=0, size=0):
    return pl.pallas_call(
        kernel,
        out_shape=shapes,
        in_specs=in_specs,
        out_specs=jax.tree.map(lambda _: pl.BlockSpec(memory_space=pltpu.VMEM), shapes),
        scratch_shapes=scratch,
        cost_estimate=pl.CostEstimate(flops=flops, bytes_accessed=size, transcendentals=0),
        compiler_params=pltpu.CompilerParams(vmem_limit_bytes=60000 * 1024),
    )


def shape(dims, dtype):
    return jax.ShapeDtypeStruct(dims, dtype)


def block_matrix(weights):
    count, size = weights.shape[0], weights.shape[1]
    rows = [
        jnp.pad(weights[block], ((0, 0), (block * size, (count - 1 - block) * size))) for block in range(count)
    ]
    return jnp.concatenate(rows, axis=0)


def complex_matrix(weights):
    real, imag = block_matrix(weights[0]), block_matrix(weights[1])
    return jnp.concatenate(
        [jnp.concatenate([real, imag], axis=1), jnp.concatenate([-imag, real], axis=1)], axis=0
    ).astype(bf16)


def shifts(value_of, axis, ways):
    return [
        lax.ppermute(value_of(shift), axis, [(i, (i + shift) % ways) for i in range(ways)])
        for shift in range(1, ways)
    ]


def local(
    sizes,
    tokens,
    gain_in,
    spectral_w1,
    spectral_b1,
    spectral_w2,
    spectral_b2,
    gain_out,
    fc1_weight,
    fc1_bias,
    fc2_weight,
    fc2_bias,
):
    rows, width, lanes = tokens.shape
    ways = lax.axis_size("chan")
    owners = lax.axis_size("rows")
    height = rows * owners
    channels = lanes * ways
    per_owner = width // 2 // owners
    me = lax.axis_index("chan").astype(jnp.int32).reshape(1)
    forward, inverse, cos, sin = (jnp.asarray(t, bf16) for t in tables(height, width, per_owner))
    half_scale = 2.0 ** math.floor(math.log2(math.sqrt(width)))
    first_scale, second_scale = 1.0 / half_scale, half_scale / math.sqrt(width * height)

    ring_x, per_x = 4, owners // 4
    place = lax.axis_index("rows")
    pieces = 2 * ring_x
    record = jnp.concatenate(
        [
            fc1_weight.T,
            fc2_weight,
            jnp.pad(fc1_bias[:, None], ((0, 0), (0, lanes - 1))),
        ],
        axis=1,
    )
    units = record.shape[0] // pieces
    mine = lax.dynamic_slice_in_dim(
        record, ((place // per_x) * 2 + place % 2) * units, units, axis=0
    )
    stage = jnp.concatenate([mine] + shifts(lambda s: mine, "chan", ways), axis=0)
    parts = [stage]
    for shift in range(1, ring_x):
        parts.append(
            lax.ppermute(stage, "rows", [(i, (i + shift * per_x) % owners) for i in range(owners)])
        )
    near = jnp.concatenate(parts, axis=0)
    far = lax.ppermute(near, "rows", [(i, i ^ 1) for i in range(owners)])

    stats = call(stats_kernel, shape((3, rows, width), f32), vmem(2))(
        tokens, fc2_bias.astype(f32).reshape(1, lanes)
    )
    others = shifts(lambda s: stats, "chan", ways)
    spectra, resid = call(
        partial(forward_kernel, channels, first_scale),
        (shape((owners, rows, 2 * per_owner, lanes), bf16), shape((rows, width, lanes), f32)),
        vmem(7),
    )(tokens, stats, *others, gain_in.reshape(1, lanes), forward)
    columns = lax.all_to_all(spectra, "rows", split_axis=0, concat_axis=0)
    total = owners * rows * 2 * per_owner
    back = call(
        partial(column_kernel, second_scale),
        shape((total, lanes), bf16),
        vmem(7),
        scratch=[
            pltpu.VMEM((total, lanes), f32),
            pltpu.VMEM((height, per_owner * lanes), bf16),
            pltpu.VMEM((height, per_owner * lanes), bf16),
        ],
    )(
        columns.reshape(total, lanes),
        cos,
        sin,
        complex_matrix(spectral_w1),
        spectral_b1.reshape(1, -1),
        complex_matrix(spectral_w2),
        spectral_b2.reshape(1, -1),
    )
    returned = lax.all_to_all(
        back.reshape(owners, rows, 2 * per_owner, lanes), "rows", split_axis=0, concat_axis=0
    )
    share = rows // ways * width
    mixed = call(
        partial(inverse_kernel, first_scale),
        [shape((share, lanes), bf16)] * ways,
        [smem] + vmem(3),
    )(me, returned, inverse, resid)
    whole = [mixed[0]] + shifts(lambda s: mixed[s], "chan", ways)
    result = call(
        partial(mlp_kernel, 256),
        [shape((share, lanes), bf16)] * ways,
        [smem] + vmem(11),
        scratch=[
            pltpu.VMEM((ways, share, lanes), bf16),
            pltpu.VMEM((ways, share, lanes), bf16),
            pltpu.VMEM((ways, lanes), f32),
        ],
    )(me, *whole, near, far, gain_out.reshape(1, channels), stats, *others)
    final = jnp.zeros((ways, share, lanes), bf16)
    for shift, part in enumerate([result[0]] + shifts(lambda s: result[s], "chan", ways)):
        final = lax.dynamic_update_slice(
            final, part[None], (lax.rem(me[0] + ways - shift, ways), 0, 0)
        )
    return final.reshape(rows, width, lanes)


def solution(mesh):
    return jax.shard_map(
        partial(local, dict(mesh.shape)),
        mesh=mesh,
        in_specs=(
            P("rows", None, "chan"),
            P("chan"),
            P(None, "chan", None, None),
            P(None, "chan", None),
            P(None, "chan", None, None),
            P(None, "chan", None),
            P(),
            P(None, "chan"),
            P("chan"),
            P("chan", None),
            P("chan"),
        ),
        out_specs=P("rows", None, "chan"),
        check_vma=False,
    )
```

```python
import math
from functools import partial

import jax
import jax.numpy as jnp
import numpy as np
from jax import lax
from jax.experimental import pallas as pl
from jax.experimental.pallas import tpu as pltpu
from jax.sharding import PartitionSpec as P

norm_eps = 1e-05
shrink_level = 0.01
bf16 = jnp.bfloat16
f32 = jnp.float32


def tables(rows, width, per_owner):
    owners = width // 2 // per_owner
    place = np.arange(width)
    freq = np.arange(width // 2).reshape(owners, 1, per_owner)
    freq = np.broadcast_to(freq, (owners, 2, per_owner)).reshape(-1)
    part = np.broadcast_to(np.arange(2).reshape(1, 2, 1), (owners, 2, per_owner)).reshape(-1)
    angle = 2.0 * np.pi / width * ((freq[:, None] * place[None, :]) % width)
    forward = np.where(part[:, None] == 0, np.cos(angle), -np.sin(angle))
    inverse = (forward * np.where(freq == 0, 1.0, 2.0)[:, None]).T
    grid = np.arange(rows)
    turn = 2.0 * np.pi / rows * ((grid[:, None] * grid[None, :]) % rows)
    return forward, inverse, np.cos(turn), np.sin(turn)


def mm(left, right):
    return jnp.dot(left, right, preferred_element_type=f32)


def mm_t(left, right):
    return lax.dot_general(left, right, (((1,), (1,)), ((), ())), preferred_element_type=f32)


def stats_kernel(x_ref, bias_ref, o_ref):
    rows, width, lanes = x_ref.shape
    o_ref[2] = jnp.zeros((rows, width), f32)
    o_ref[2, 0:1, 0:lanes] = bias_ref[...].astype(f32)
    ones = jnp.ones((8, x_ref.shape[2]), bf16)
    for row in range(rows):
        x = x_ref[row]
        wide = x.astype(f32)
        square = wide * wide
        high = square.astype(bf16)
        low = (square - high.astype(f32)).astype(bf16)
        o_ref[0, row : row + 1, :] = mm_t(ones, x)[0:1]
        o_ref[1, row : row + 1, :] = (mm_t(ones, high) + mm_t(ones, low))[0:1]


def forward_kernel(channels, scale, x_ref, s0_ref, s1_ref, s2_ref, s3_ref, gain_ref, table_hbm, o_ref, f_ref, table_ref, sem):
    rows, _, lanes = x_ref.shape
    fetch = pltpu.make_async_copy(table_hbm, table_ref, sem)
    fetch.start()
    owners = o_ref.shape[0]
    total = (s0_ref[0] + s1_ref[0]) + (s2_ref[0] + s3_ref[0])
    square = (s0_ref[1] + s1_ref[1]) + (s2_ref[1] + s3_ref[1])
    center = total / channels
    spread = square / channels - center * center
    flipped = jnp.transpose(jnp.concatenate([center, lax.rsqrt(spread + norm_eps)], axis=0))
    f_ref[...] = flipped
    gain = gain_ref[...]
    for pair in range(rows // 2):
        sides = []
        for row in (2 * pair, 2 * pair + 1):
            x = x_ref[row].astype(f32)
            normed = (x - flipped[:, row : row + 1]) * flipped[:, rows + row : rows + row + 1] * gain
            sides.append(normed.astype(bf16))
        if pair == 0:
            fetch.wait()
        out = mm(table_ref[...], jnp.concatenate(sides, axis=1)) * scale
        for side in range(2):
            o_ref[:, 2 * pair + side] = (
                out[:, side * lanes : (side + 1) * lanes].reshape(owners, -1, lanes).astype(bf16)
            )


def soften(values):
    return jnp.where(
        values > shrink_level,
        values - shrink_level,
        jnp.where(values < -shrink_level, values + shrink_level, 0.0),
    )


def block_matrix(w_ref, part):
    count, size = w_ref.shape[1], w_ref.shape[2]
    rows = []
    for block in range(count):
        cells = [jnp.zeros((size, size), f32)] * count
        cells[block] = w_ref[part, block]
        rows.append(jnp.concatenate(cells, axis=1))
    return jnp.concatenate(rows, axis=0)


def complex_matrix(w_ref):
    real, imag = block_matrix(w_ref, 0), block_matrix(w_ref, 1)
    return jnp.concatenate(
        [jnp.concatenate([real, imag], axis=1), jnp.concatenate([-imag, real], axis=1)], axis=0
    ).astype(bf16)


def bias_row(b_ref):
    parts, count = b_ref.shape[0], b_ref.shape[1]
    return jnp.concatenate(
        [b_ref[part, block : block + 1, :] for part in range(parts) for block in range(count)], axis=1
    )


def column_kernel(
    scale,
    x_ref,
    cos_hbm,
    sin_hbm,
    w1_ref,
    b1_ref,
    w2_ref,
    b2_ref,
    o_ref,
    wide_ref,
    real_ref,
    imag_ref,
    cos_ref,
    sin_ref,
    sems,
):
    fetches = [
        pltpu.make_async_copy(source, target, sems.at[place])
        for place, (source, target) in enumerate(((cos_hbm, cos_ref), (sin_hbm, sin_ref)))
    ]
    for fetch in fetches:
        fetch.start()
    weight_one, weight_two = complex_matrix(w1_ref), complex_matrix(w2_ref)
    bias_one, bias_two = bias_row(b1_ref), bias_row(b2_ref)
    height = cos_ref.shape[0]
    lanes = x_ref.shape[1]
    step = x_ref.shape[0] // height
    count = step // 2
    wide_ref[...] = x_ref[...].astype(f32)
    for part, target in ((0, real_ref), (1, imag_ref)):
        for k in range(count):
            target[:, k * lanes : (k + 1) * lanes] = wide_ref[
                pl.ds(part * count + k, height, stride=step), :
            ].astype(bf16)
    for fetch in fetches:
        fetch.wait()
    for half in range(count // 2):
        span = pl.ds(half * 2 * lanes, 2 * lanes)
        cos, sin = cos_ref[...], sin_ref[...]
        real, imag = real_ref[:, span], imag_ref[:, span]
        out_real = (mm(cos, real) + mm(sin, imag)) * scale
        out_imag = (mm(cos, imag) - mm(sin, real)) * scale
        next_real, next_imag = [], []
        for side in range(2):
            cut = slice(side * lanes, (side + 1) * lanes)
            both = jnp.concatenate([out_real[:, cut].astype(bf16), out_imag[:, cut].astype(bf16)], axis=1)
            first = jnp.maximum(mm(both, weight_one) + bias_one, 0.0).astype(bf16)
            second = soften(mm(first, weight_two) + bias_two).astype(bf16)
            next_real.append(second[:, :lanes])
            next_imag.append(second[:, lanes:])
        real, imag = jnp.concatenate(next_real, axis=1), jnp.concatenate(next_imag, axis=1)
        back_real = (mm(cos, real) - mm(sin, imag)) * scale
        back_imag = (mm(cos, imag) + mm(sin, real)) * scale
        for side in range(2):
            cut = slice(side * lanes, (side + 1) * lanes)
            k = half * 2 + side
            wide_ref[pl.ds(k, height, stride=step), :] = back_real[:, cut]
            wide_ref[pl.ds(count + k, height, stride=step), :] = back_imag[:, cut]
    o_ref[...] = wide_ref[...].astype(bf16)


def inverse_kernel(scale, me_ref, x_ref, table_hbm, t_ref, f_ref, gain_ref, *refs):
    *o_refs, table_ref, sem = refs
    fetch = pltpu.make_async_copy(table_hbm, table_ref, sem)
    fetch.start()
    ways = len(o_refs)
    rows, width, lanes = t_ref.shape
    group = rows // ways
    me = me_ref[0]
    gain = gain_ref[...]
    column = lax.broadcasted_iota(jnp.int32, f_ref.shape, 1)
    for shift in range(ways):
        owner = lax.rem(me + shift, ways)
        for pair in range(group // 2):
            first = owner * group + 2 * pair
            sides = [
                x_ref[:, first + side].astype(f32).reshape(-1, lanes).astype(bf16) for side in range(2)
            ]
            if shift == 0 and pair == 0:
                fetch.wait()
            out = mm(table_ref[...], jnp.concatenate(sides, axis=1)) * scale
            for side in range(2):
                row = first + side
                source = t_ref[row].astype(f32)
                center = jnp.sum(jnp.where(column == row, f_ref[...], 0.0), axis=1, keepdims=True)
                factor = jnp.sum(jnp.where(column == row + rows, f_ref[...], 0.0), axis=1, keepdims=True)
                normed = (source - center) * factor * gain
                o_refs[shift][pl.ds((2 * pair + side) * width, width), :] = (
                    (out[:, side * lanes : (side + 1) * lanes] + normed) + source
                ).astype(bf16)


def gelu(values):
    return 0.5 * values * (1.0 + lax.erf(values * math.sqrt(0.5)))


def mlp_kernel(tile, me_ref, x0, x1, x2, x3, wa_ref, wb_ref, gain_ref, s0, s1, s2, s3, y0, y1, y2, y3, x_ref, y_ref, b_ref):
    ways, tokens, lanes = x_ref.shape
    channels = ways * lanes
    me = me_ref[0]
    biases_out = (s0, s1, s2, s3)
    for shift, ref in enumerate((x0, x1, x2, x3)):
        x_ref[lax.rem(me + ways - shift, ways)] = ref[...]
        b_ref[pl.ds(lax.rem(me + ways - shift, ways), 1), :] = biases_out[shift][2, 0:1, 0:lanes]
    unit = jnp.ones((8, lanes), bf16)
    hidden_block = 512
    biases = []
    for ref in (wa_ref, wb_ref):
        for start in range(0, ref.shape[0], hidden_block):
            biases.append(mm_t(unit, ref[start : start + hidden_block, 2 * channels :])[0:1])

    def body(index, carry):
        span = pl.ds(pl.multiple_of(index * tile, tile), tile)
        mixed = [x_ref[block, span, :].astype(f32) for block in range(ways)]
        total = sum(mixed[1:], mixed[0])
        square = sum((m * m for m in mixed[1:]), mixed[0] * mixed[0])
        center = jnp.sum(total, axis=1, keepdims=True) / channels
        spread = jnp.sum(square, axis=1, keepdims=True) / channels - center * center
        inverse = lax.rsqrt(spread + norm_eps)
        normed = jnp.concatenate(
            [
                ((m - center) * inverse * gain_ref[:, b * lanes : (b + 1) * lanes]).astype(bf16)
                for b, m in enumerate(mixed)
            ],
            axis=1,
        )
        acc = None
        block = 0
        for ref in (wa_ref, wb_ref):
            for start in range(0, ref.shape[0], hidden_block):
                rows = pl.ds(start, hidden_block)
                hidden = gelu(mm_t(normed, ref[rows, :channels]) + biases[block]).astype(bf16)
                product = mm(hidden, ref[rows, channels : 2 * channels])
                acc = product if acc is None else acc + product
                block += 1
        for b in range(ways):
            cut = slice(b * lanes, (b + 1) * lanes)
            y_ref[b, span, :] = (mixed[b] + acc[:, cut] + b_ref[b : b + 1, :]).astype(bf16)
        return carry

    lax.fori_loop(0, tokens // tile, body, 0)
    for shift, ref in enumerate((y0, y1, y2, y3)):
        ref[...] = y_ref[lax.rem(me + shift, ways)]


def place_kernel(me_ref, x0, x1, x2, x3, o_ref):
    ways = o_ref.shape[0]
    for shift, ref in enumerate((x0, x1, x2, x3)):
        o_ref[lax.rem(me_ref[0] + ways - shift, ways)] = ref[...]


def piece_kernel(piece_ref, one_ref, bias_ref, two_ref, o_ref, flat_ref):
    units, columns = o_ref.shape
    channels = one_ref.shape[0]
    lanes = columns - 2 * channels
    piece = piece_ref[0]
    slab = pl.ds(pl.multiple_of(piece * units // lanes * lanes, lanes), lanes)
    row = lax.broadcasted_iota(jnp.int32, (lanes, lanes), 0)
    column = lax.broadcasted_iota(jnp.int32, (lanes, lanes), 1)
    unit = jnp.where(row == column, 1.0, 0.0).astype(bf16)
    flat_ref[:, 0:channels] = mm_t(unit, one_ref[:, slab])
    bias = jnp.where(row == column, jnp.broadcast_to(bias_ref[:, slab].astype(f32), (lanes, lanes)), 0.0)
    flat_ref[:, channels:] = bias
    within = pl.ds(pl.multiple_of(lax.rem(piece * units, lanes), units), units)
    o_ref[:, 0:channels] = flat_ref[within, 0:channels].astype(bf16)
    o_ref[:, channels : 2 * channels] = two_ref[pl.ds(pl.multiple_of(piece * units, units), units), :]
    o_ref[:, 2 * channels :] = flat_ref[within, channels:].astype(bf16)


def vmem(count):
    return [pl.BlockSpec(memory_space=pltpu.VMEM)] * count


smem = pl.BlockSpec(memory_space=pltpu.SMEM)
hbm = pl.BlockSpec(memory_space=pltpu.HBM)


def call(kernel, shapes, in_specs, scratch=(), flops=0, size=0):
    return pl.pallas_call(
        kernel,
        out_shape=shapes,
        in_specs=in_specs,
        out_specs=jax.tree.map(lambda _: pl.BlockSpec(memory_space=pltpu.VMEM), shapes),
        scratch_shapes=scratch,
        cost_estimate=pl.CostEstimate(flops=flops, bytes_accessed=size, transcendentals=0),
        compiler_params=pltpu.CompilerParams(vmem_limit_bytes=24 * 1024 * 1024),
    )


def shape(dims, dtype):
    return jax.ShapeDtypeStruct(dims, dtype)


def shifts(value_of, axis, ways):
    return [
        lax.ppermute(value_of(shift), axis, [(i, (i + shift) % ways) for i in range(ways)])
        for shift in range(1, ways)
    ]


def local(
    tokens,
    gain_in,
    spectral_w1,
    spectral_b1,
    spectral_w2,
    spectral_b2,
    gain_out,
    fc1_weight,
    fc1_bias,
    fc2_weight,
    fc2_bias,
):
    rows, width, lanes = tokens.shape
    ways = lax.axis_size("chan")
    owners = lax.axis_size("rows")
    height = rows * owners
    channels = lanes * ways
    per_owner = width // 2 // owners
    me = lax.axis_index("chan").astype(jnp.int32).reshape(1)
    forward, inverse, cos, sin = (jnp.asarray(t, bf16) for t in tables(height, width, per_owner))
    half_scale = 2.0 ** math.floor(math.log2(math.sqrt(width)))
    first_scale, second_scale = 1.0 / half_scale, half_scale / math.sqrt(width * height)

    stats = call(stats_kernel, shape((3, rows, width), f32), vmem(2))(
        tokens, fc2_bias.reshape(1, lanes)
    )
    others = shifts(lambda s: stats, "chan", ways)
    spectra, flipped = call(
        partial(forward_kernel, channels, first_scale),
        (shape((owners, rows, 2 * per_owner, lanes), bf16), shape((width, 2 * rows), f32)),
        vmem(6) + [hbm],
        scratch=[pltpu.VMEM(forward.shape, bf16), pltpu.SemaphoreType.DMA],
    )(tokens, stats, *others, gain_in.reshape(1, lanes), forward)
    columns = lax.all_to_all(spectra, "rows", split_axis=0, concat_axis=0)

    ring_x, per_x = 4, owners // 4
    place = lax.axis_index("rows").astype(jnp.int32)
    units = fc1_weight.shape[1] // (2 * ring_x)
    piece = ((place // per_x) * 2 + place % 2).reshape(1)
    mine = call(
        piece_kernel,
        shape((units, 2 * channels + lanes), bf16),
        [smem] + vmem(3),
        scratch=[pltpu.VMEM((lanes, channels + lanes), f32)],
    )(piece, fc1_weight, fc1_bias.reshape(1, -1), fc2_weight)
    stage = jnp.concatenate([mine] + shifts(lambda s: mine, "chan", ways), axis=0)
    parts = [stage]
    for shift in range(1, ring_x):
        parts.append(
            lax.ppermute(stage, "rows", [(i, (i + shift * per_x) % owners) for i in range(owners)])
        )
    near = jnp.concatenate(parts, axis=0)
    far = lax.ppermute(near, "rows", [(i, i ^ 1) for i in range(owners)])

    total = owners * rows * 2 * per_owner
    back = call(
        partial(column_kernel, second_scale),
        shape((total, lanes), bf16),
        vmem(1) + [hbm] * 2 + vmem(4),
        scratch=[
            pltpu.VMEM((total, lanes), f32),
            pltpu.VMEM((height, per_owner * lanes), bf16),
            pltpu.VMEM((height, per_owner * lanes), bf16),
            pltpu.VMEM(cos.shape, bf16),
            pltpu.VMEM(sin.shape, bf16),
            pltpu.SemaphoreType.DMA((2,)),
        ],
    )(
        columns.reshape(total, lanes),
        cos,
        sin,
        spectral_w1,
        spectral_b1,
        spectral_w2,
        spectral_b2,
    )
    returned = lax.all_to_all(
        back.reshape(owners, rows, 2 * per_owner, lanes), "rows", split_axis=0, concat_axis=0
    )
    share = rows // ways * width
    mixed = call(
        partial(inverse_kernel, first_scale),
        [shape((share, lanes), bf16)] * ways,
        [smem] + vmem(1) + [hbm] + vmem(3),
        scratch=[pltpu.VMEM(inverse.shape, bf16), pltpu.SemaphoreType.DMA],
    )(me, returned, inverse, tokens, flipped, gain_in.reshape(1, lanes))
    whole = [mixed[0]] + shifts(lambda s: mixed[s], "chan", ways)
    result = call(
        partial(mlp_kernel, 256),
        [shape((share, lanes), bf16)] * ways,
        [smem] + vmem(11),
        scratch=[
            pltpu.VMEM((ways, share, lanes), bf16),
            pltpu.VMEM((ways, share, lanes), bf16),
            pltpu.VMEM((ways, lanes), f32),
        ],
    )(me, *whole, near, far, gain_out.reshape(1, channels), stats, *others)
    parts = [result[0]] + shifts(lambda s: result[s], "chan", ways)
    final = call(place_kernel, shape((ways, share, lanes), bf16), [smem] + vmem(4))(me, *parts)
    return final.reshape(rows, width, lanes)


def solution(mesh):
    return jax.shard_map(
        local,
        mesh=mesh,
        in_specs=(
            P("rows", None, "chan"),
            P("chan"),
            P(None, "chan", None, None),
            P(None, "chan", None),
            P(None, "chan", None, None),
            P(None, "chan", None),
            P(),
            P(None, "chan"),
            P("chan"),
            P("chan", None),
            P("chan"),
        ),
        out_specs=P("rows", None, "chan"),
        check_vma=False,
    )
```

```python
import math
from functools import partial

import jax
import jax.numpy as jnp
import numpy as np
from jax import lax
from jax.experimental import pallas as pl
from jax.experimental.pallas import tpu as pltpu
from jax.sharding import PartitionSpec as P

norm_eps = 1e-05
shrink_level = 0.01
bf16 = jnp.bfloat16
f32 = jnp.float32


def tables(rows, width, per_owner):
    owners = width // 2 // per_owner
    place = np.arange(width)
    freq = np.arange(width // 2).reshape(owners, 1, per_owner)
    freq = np.broadcast_to(freq, (owners, 2, per_owner)).reshape(-1)
    part = np.broadcast_to(np.arange(2).reshape(1, 2, 1), (owners, 2, per_owner)).reshape(-1)
    angle = 2.0 * np.pi / width * ((freq[:, None] * place[None, :]) % width)
    forward = np.where(part[:, None] == 0, np.cos(angle), -np.sin(angle))
    inverse = (forward * np.where(freq == 0, 1.0, 2.0)[:, None]).T
    grid = np.arange(rows)
    turn = 2.0 * np.pi / rows * ((grid[:, None] * grid[None, :]) % rows)
    return forward, inverse, np.cos(turn), np.sin(turn)


def mm(left, right):
    return jnp.dot(left, right, preferred_element_type=f32)


def mm_t(left, right):
    return lax.dot_general(left, right, (((1,), (1,)), ((), ())), preferred_element_type=f32)


def stats_kernel(x_ref, bias_ref, o_ref):
    rows, width, lanes = x_ref.shape
    o_ref[2] = jnp.zeros((rows, width), f32)
    o_ref[2, 0:1, 0:lanes] = bias_ref[...].astype(f32)
    ones = jnp.ones((8, x_ref.shape[2]), bf16)
    for row in range(rows):
        x = x_ref[row]
        wide = x.astype(f32)
        square = wide * wide
        high = square.astype(bf16)
        low = (square - high.astype(f32)).astype(bf16)
        o_ref[0, row : row + 1, :] = mm_t(ones, x)[0:1]
        o_ref[1, row : row + 1, :] = (mm_t(ones, high) + mm_t(ones, low))[0:1]


def forward_kernel(channels, scale, x_ref, s0_ref, s1_ref, s2_ref, s3_ref, gain_ref, table_hbm, o_ref, f_ref, table_ref, sem):
    rows, _, lanes = x_ref.shape
    fetch = pltpu.make_async_copy(table_hbm, table_ref, sem)
    fetch.start()
    owners = o_ref.shape[0]
    total = (s0_ref[0] + s1_ref[0]) + (s2_ref[0] + s3_ref[0])
    square = (s0_ref[1] + s1_ref[1]) + (s2_ref[1] + s3_ref[1])
    center = total / channels
    spread = square / channels - center * center
    flipped = jnp.transpose(jnp.concatenate([center, lax.rsqrt(spread + norm_eps)], axis=0))
    f_ref[...] = flipped
    gain = gain_ref[...]
    for pair in range(rows // 2):
        sides = []
        for row in (2 * pair, 2 * pair + 1):
            x = x_ref[row].astype(f32)
            normed = (x - flipped[:, row : row + 1]) * flipped[:, rows + row : rows + row + 1] * gain
            sides.append(normed.astype(bf16))
        if pair == 0:
            fetch.wait()
        out = mm(table_ref[...], jnp.concatenate(sides, axis=1)) * scale
        for side in range(2):
            o_ref[:, 2 * pair + side] = (
                out[:, side * lanes : (side + 1) * lanes].reshape(owners, -1, lanes).astype(bf16)
            )


def soften(values):
    return jnp.where(
        values > shrink_level,
        values - shrink_level,
        jnp.where(values < -shrink_level, values + shrink_level, 0.0),
    )


def block_matrix(w_ref, part):
    count, size = w_ref.shape[1], w_ref.shape[2]
    rows = []
    for block in range(count):
        cells = [jnp.zeros((size, size), f32)] * count
        cells[block] = w_ref[part, block]
        rows.append(jnp.concatenate(cells, axis=1))
    return jnp.concatenate(rows, axis=0)


def complex_matrix(w_ref):
    real, imag = block_matrix(w_ref, 0), block_matrix(w_ref, 1)
    return jnp.concatenate(
        [jnp.concatenate([real, imag], axis=1), jnp.concatenate([-imag, real], axis=1)], axis=0
    ).astype(bf16)


def bias_row(b_ref):
    parts, count = b_ref.shape[0], b_ref.shape[1]
    return jnp.concatenate(
        [b_ref[part, block : block + 1, :] for part in range(parts) for block in range(count)], axis=1
    )


def column_kernel(
    scale,
    x_ref,
    cos_hbm,
    sin_hbm,
    w1_ref,
    b1_ref,
    w2_ref,
    b2_ref,
    o_ref,
    wide_ref,
    real_ref,
    imag_ref,
    cos_ref,
    sin_ref,
    sems,
):
    fetches = [
        pltpu.make_async_copy(source, target, sems.at[place])
        for place, (source, target) in enumerate(((cos_hbm, cos_ref), (sin_hbm, sin_ref)))
    ]
    for fetch in fetches:
        fetch.start()
    weight_one, weight_two = complex_matrix(w1_ref), complex_matrix(w2_ref)
    bias_one, bias_two = bias_row(b1_ref), bias_row(b2_ref)
    height = cos_ref.shape[0]
    lanes = x_ref.shape[1]
    step = x_ref.shape[0] // height
    count = step // 2
    wide_ref[...] = x_ref[...].astype(f32)
    for part, target in ((0, real_ref), (1, imag_ref)):
        for k in range(count):
            target[:, k * lanes : (k + 1) * lanes] = wide_ref[
                pl.ds(part * count + k, height, stride=step), :
            ].astype(bf16)
    for fetch in fetches:
        fetch.wait()
    for half in range(count // 2):
        span = pl.ds(half * 2 * lanes, 2 * lanes)
        cos, sin = cos_ref[...], sin_ref[...]
        real, imag = real_ref[:, span], imag_ref[:, span]
        out_real = (mm(cos, real) + mm(sin, imag)) * scale
        out_imag = (mm(cos, imag) - mm(sin, real)) * scale
        next_real, next_imag = [], []
        for side in range(2):
            cut = slice(side * lanes, (side + 1) * lanes)
            both = jnp.concatenate([out_real[:, cut].astype(bf16), out_imag[:, cut].astype(bf16)], axis=1)
            first = jnp.maximum(mm(both, weight_one) + bias_one, 0.0).astype(bf16)
            second = soften(mm(first, weight_two) + bias_two).astype(bf16)
            next_real.append(second[:, :lanes])
            next_imag.append(second[:, lanes:])
        real, imag = jnp.concatenate(next_real, axis=1), jnp.concatenate(next_imag, axis=1)
        back_real = (mm(cos, real) - mm(sin, imag)) * scale
        back_imag = (mm(cos, imag) + mm(sin, real)) * scale
        for side in range(2):
            cut = slice(side * lanes, (side + 1) * lanes)
            k = half * 2 + side
            wide_ref[pl.ds(k, height, stride=step), :] = back_real[:, cut]
            wide_ref[pl.ds(count + k, height, stride=step), :] = back_imag[:, cut]
    o_ref[...] = wide_ref[...].astype(bf16)


def inverse_kernel(scale, me_ref, x_ref, table_hbm, t_ref, f_ref, gain_ref, *refs):
    *o_refs, table_ref, sem = refs
    fetch = pltpu.make_async_copy(table_hbm, table_ref, sem)
    fetch.start()
    ways = len(o_refs) // 2
    rows, width, lanes = t_ref.shape
    group = rows // ways
    me = me_ref[0]
    gain = gain_ref[...]
    column = lax.broadcasted_iota(jnp.int32, f_ref.shape, 1)
    for shift in range(ways):
        owner = lax.rem(me + shift, ways)
        for pair in range(group // 2):
            first = owner * group + 2 * pair
            sides = [
                x_ref[:, first + side].astype(f32).reshape(-1, lanes).astype(bf16) for side in range(2)
            ]
            if shift == 0 and pair == 0:
                fetch.wait()
            out = mm(table_ref[...], jnp.concatenate(sides, axis=1)) * scale
            for side in range(2):
                row = first + side
                source = t_ref[row].astype(f32)
                center = jnp.sum(jnp.where(column == row, f_ref[...], 0.0), axis=1, keepdims=True)
                factor = jnp.sum(jnp.where(column == row + rows, f_ref[...], 0.0), axis=1, keepdims=True)
                normed = (source - center) * factor * gain
                o_refs[side * ways + shift][pl.ds(pair * width, width), :] = (
                    (out[:, side * lanes : (side + 1) * lanes] + normed) + source
                ).astype(bf16)


def gelu(values):
    return 0.5 * values * (1.0 + lax.erf(values * math.sqrt(0.5)))


def mlp_kernel(tile, me_ref, x0, x1, x2, x3, wa_ref, wb_ref, gain_ref, s0, s1, s2, s3, y0, y1, y2, y3, x_ref, y_ref, b_ref):
    ways, tokens, lanes = x_ref.shape
    channels = ways * lanes
    me = me_ref[0]
    biases_out = (s0, s1, s2, s3)
    for shift, ref in enumerate((x0, x1, x2, x3)):
        x_ref[lax.rem(me + ways - shift, ways)] = ref[...]
        b_ref[pl.ds(lax.rem(me + ways - shift, ways), 1), :] = biases_out[shift][2, 0:1, 0:lanes]
    unit = jnp.ones((8, lanes), bf16)
    hidden_block = 512
    biases = []
    for ref in (wa_ref, wb_ref):
        for start in range(0, ref.shape[0], hidden_block):
            biases.append(mm_t(unit, ref[start : start + hidden_block, 2 * channels :])[0:1])

    def body(index, carry):
        span = pl.ds(pl.multiple_of(index * tile, tile), tile)
        mixed = [x_ref[block, span, :].astype(f32) for block in range(ways)]
        total = sum(mixed[1:], mixed[0])
        square = sum((m * m for m in mixed[1:]), mixed[0] * mixed[0])
        center = jnp.sum(total, axis=1, keepdims=True) / channels
        spread = jnp.sum(square, axis=1, keepdims=True) / channels - center * center
        inverse = lax.rsqrt(spread + norm_eps)
        normed = jnp.concatenate(
            [
                ((m - center) * inverse * gain_ref[:, b * lanes : (b + 1) * lanes]).astype(bf16)
                for b, m in enumerate(mixed)
            ],
            axis=1,
        )
        acc = None
        block = 0
        for ref in (wa_ref, wb_ref):
            for start in range(0, ref.shape[0], hidden_block):
                rows = pl.ds(start, hidden_block)
                hidden = gelu(mm_t(normed, ref[rows, :channels]) + biases[block]).astype(bf16)
                product = mm(hidden, ref[rows, channels : 2 * channels])
                acc = product if acc is None else acc + product
                block += 1
        for b in range(ways):
            cut = slice(b * lanes, (b + 1) * lanes)
            y_ref[b, span, :] = (mixed[b] + acc[:, cut] + b_ref[b : b + 1, :]).astype(bf16)
        return carry

    lax.fori_loop(0, tokens // tile, body, 0)
    for shift, ref in enumerate((y0, y1, y2, y3)):
        ref[...] = y_ref[lax.rem(me + shift, ways)]


def place_kernel(me_ref, *refs):
    *parts, o_ref = refs
    ways = o_ref.shape[0]
    half = o_ref.shape[1] // 2
    for place, part in enumerate(parts):
        shift = place % ways
        o_ref[lax.rem(me_ref[0] + ways - shift, ways), pl.ds(place // ways * half, half), :] = part[...]


def piece_kernel(piece_ref, one_ref, bias_ref, two_ref, o_ref, flat_ref):
    channels = one_ref.shape[0]
    units = o_ref.shape[0] // 2
    lanes = o_ref.shape[1] - 2 * channels
    row = lax.broadcasted_iota(jnp.int32, (lanes, lanes), 0)
    column = lax.broadcasted_iota(jnp.int32, (lanes, lanes), 1)
    unit = jnp.where(row == column, 1.0, 0.0).astype(bf16)
    for half in range(2):
        first = half * (one_ref.shape[1] // 2) + piece_ref[half] * units
        slab = pl.ds(pl.multiple_of(first // lanes * lanes, lanes), lanes)
        bias = jnp.broadcast_to(bias_ref[:, slab].astype(f32), (lanes, lanes))
        flat_ref[:, 0:channels] = mm_t(unit, one_ref[:, slab])
        flat_ref[:, channels:] = jnp.where(row == column, bias, 0.0)
        within = pl.ds(pl.multiple_of(lax.rem(first, lanes), units), units)
        target = pl.ds(half * units, units)
        o_ref[target, 0:channels] = flat_ref[within, 0:channels].astype(bf16)
        o_ref[target, channels : 2 * channels] = two_ref[pl.ds(pl.multiple_of(first, units), units), :]
        o_ref[target, 2 * channels :] = flat_ref[within, channels:].astype(bf16)


def split_kernel(*refs):
    *parts, first_ref, second_ref = refs
    size = parts[0].shape[0] // 2
    for place, part in enumerate(parts):
        for half, ref in enumerate((first_ref, second_ref)):
            ref[place * size : (place + 1) * size, :] = part[half * size : (half + 1) * size, :]


def join_kernel(*refs):
    *parts, after_ref, o_ref = refs
    start = 0
    for part in parts:
        o_ref[start : start + part.shape[0], :] = part[...]
        start += part.shape[0]


def vmem(count):
    return [pl.BlockSpec(memory_space=pltpu.VMEM)] * count


smem = pl.BlockSpec(memory_space=pltpu.SMEM)
hbm = pl.BlockSpec(memory_space=pltpu.HBM)


def call(kernel, shapes, in_specs, scratch=(), flops=0, size=0):
    return pl.pallas_call(
        kernel,
        out_shape=shapes,
        in_specs=in_specs,
        out_specs=jax.tree.map(lambda _: pl.BlockSpec(memory_space=pltpu.VMEM), shapes),
        scratch_shapes=scratch,
        cost_estimate=pl.CostEstimate(flops=flops, bytes_accessed=size, transcendentals=0),
        compiler_params=pltpu.CompilerParams(vmem_limit_bytes=24 * 1024 * 1024),
    )


def shape(dims, dtype):
    return jax.ShapeDtypeStruct(dims, dtype)


def shifts(value_of, axis, ways):
    return [
        lax.ppermute(value_of(shift), axis, [(i, (i + shift) % ways) for i in range(ways)])
        for shift in range(1, ways)
    ]


def local(
    tokens,
    gain_in,
    spectral_w1,
    spectral_b1,
    spectral_w2,
    spectral_b2,
    gain_out,
    fc1_weight,
    fc1_bias,
    fc2_weight,
    fc2_bias,
):
    rows, width, lanes = tokens.shape
    ways = lax.axis_size("chan")
    owners = lax.axis_size("rows")
    height = rows * owners
    channels = lanes * ways
    per_owner = width // 2 // owners
    me = lax.axis_index("chan").astype(jnp.int32).reshape(1)
    forward, inverse, cos, sin = (jnp.asarray(t, bf16) for t in tables(height, width, per_owner))
    half_scale = 2.0 ** math.floor(math.log2(math.sqrt(width)))
    first_scale, second_scale = 1.0 / half_scale, half_scale / math.sqrt(width * height)

    stats = call(stats_kernel, shape((3, rows, width), f32), vmem(2))(
        tokens, fc2_bias.reshape(1, lanes)
    )
    others = shifts(lambda s: stats, "chan", ways)
    spectra, flipped = call(
        partial(forward_kernel, channels, first_scale),
        (shape((owners, rows, 2 * per_owner, lanes), bf16), shape((width, 2 * rows), f32)),
        vmem(6) + [hbm],
        scratch=[pltpu.VMEM(forward.shape, bf16), pltpu.SemaphoreType.DMA],
    )(tokens, stats, *others, gain_in.reshape(1, lanes), forward)
    columns = lax.all_to_all(spectra, "rows", split_axis=0, concat_axis=0)

    ring_x, ring_y, per_x = 4, 4, owners // 4
    place = lax.axis_index("rows").astype(jnp.int32)
    units = fc1_weight.shape[1] // (2 * ring_x)
    across, along, core = place // per_x, place // 2 % ring_y, place % 2
    piece = jnp.stack([across * 2 + core, along * 2 + core])
    mine = call(
        piece_kernel,
        shape((units, 2 * channels + lanes), bf16),
        [smem] + vmem(3),
        scratch=[pltpu.VMEM((lanes, channels + lanes), f32)],
    )(piece, fc1_weight, fc1_bias.reshape(1, -1), fc2_weight)
    stage = [mine] + shifts(lambda s: mine, "chan", ways)
    count = ways * units // 2
    sides = call(
        split_kernel, [shape((count, mine.shape[1]), bf16)] * 2, vmem(ways)
    )(*stage)
    parts = list(sides)
    for shift in range(1, ring_x):
        ring = [
            [(i, (i + shift * per_x) % owners) for i in range(owners)],
            [(i, i + 2 * ((i // 2 % ring_y + shift) % ring_y - i // 2 % ring_y)) for i in range(owners)],
        ]
        for half in range(2):
            parts.append(lax.ppermute(sides[half], "rows", ring[half]))

    total = owners * rows * 2 * per_owner
    back = call(
        partial(column_kernel, second_scale),
        shape((total, lanes), bf16),
        vmem(1) + [hbm] * 2 + vmem(4),
        scratch=[
            pltpu.VMEM((total, lanes), f32),
            pltpu.VMEM((height, per_owner * lanes), bf16),
            pltpu.VMEM((height, per_owner * lanes), bf16),
            pltpu.VMEM(cos.shape, bf16),
            pltpu.VMEM(sin.shape, bf16),
            pltpu.SemaphoreType.DMA((2,)),
        ],
    )(
        columns.reshape(total, lanes),
        cos,
        sin,
        spectral_w1,
        spectral_b1,
        spectral_w2,
        spectral_b2,
    )
    returned = lax.all_to_all(
        back.reshape(owners, rows, 2 * per_owner, lanes), "rows", split_axis=0, concat_axis=0
    )
    share = rows // ways * width // 2
    mixed = call(
        partial(inverse_kernel, first_scale),
        [shape((share, lanes), bf16)] * (2 * ways),
        [smem] + vmem(1) + [hbm] + vmem(3),
        scratch=[pltpu.VMEM(inverse.shape, bf16), pltpu.SemaphoreType.DMA],
    )(me, returned, inverse, tokens, flipped, gain_in.reshape(1, lanes))
    halves = [mixed[:ways], mixed[ways:]]
    whole_a = [halves[0][0]] + shifts(lambda s: halves[0][s], "chan", ways)
    near = call(
        join_kernel,
        shape((2 * ring_x * parts[0].shape[0], parts[0].shape[1]), bf16),
        vmem(len(parts)) + [pl.BlockSpec(memory_space=pl.ANY)],
    )(*parts, mixed[0])
    far = lax.ppermute(near, "rows", [(i, i ^ 1) for i in range(owners)])
    whole_b = [halves[1][0]] + shifts(lambda s: halves[1][s], "chan", ways)

    def mlp(whole):
        return call(
            partial(mlp_kernel, 256),
            [shape((share, lanes), bf16)] * ways,
            [smem] + vmem(11),
            scratch=[
                pltpu.VMEM((ways, share, lanes), bf16),
                pltpu.VMEM((ways, share, lanes), bf16),
                pltpu.VMEM((ways, lanes), f32),
            ],
        )(me, *whole, near, far, gain_out.reshape(1, channels), stats, *others)

    result_a = mlp(whole_a)
    parts_a = [result_a[0]] + shifts(lambda s: result_a[s], "chan", ways)
    result_b = mlp(whole_b)
    parts_b = [result_b[0]] + shifts(lambda s: result_b[s], "chan", ways)
    final = call(place_kernel, shape((ways, 2 * share, lanes), bf16), [smem] + vmem(2 * ways))(
        me, *parts_a, *parts_b
    )
    return final.reshape(rows, width, lanes)


def solution(mesh):
    return jax.shard_map(
        local,
        mesh=mesh,
        in_specs=(
            P("rows", None, "chan"),
            P("chan"),
            P(None, "chan", None, None),
            P(None, "chan", None),
            P(None, "chan", None, None),
            P(None, "chan", None),
            P(),
            P(None, "chan"),
            P("chan"),
            P("chan", None),
            P("chan"),
        ),
        out_specs=P("rows", None, "chan"),
        check_vma=False,
    )
```

```python
import math
from functools import partial

import jax
import jax.numpy as jnp
import numpy as np
from jax import lax
from jax.experimental import pallas as pl
from jax.experimental.pallas import tpu as pltpu
from jax.sharding import PartitionSpec as P

norm_eps = 1e-05
shrink_level = 0.01
bf16 = jnp.bfloat16
f32 = jnp.float32


def tables(rows, width, per_owner):
    owners = width // 2 // per_owner
    place = np.arange(width)
    freq = np.arange(width // 2).reshape(owners, 1, per_owner)
    freq = np.broadcast_to(freq, (owners, 2, per_owner)).reshape(-1)
    part = np.broadcast_to(np.arange(2).reshape(1, 2, 1), (owners, 2, per_owner)).reshape(-1)
    angle = 2.0 * np.pi / width * ((freq[:, None] * place[None, :]) % width)
    forward = np.where(part[:, None] == 0, np.cos(angle), -np.sin(angle))
    grid = np.arange(rows)
    turn = 2.0 * np.pi / rows * ((grid[:, None] * grid[None, :]) % rows)
    return forward, np.cos(turn), np.sin(turn)


def mm(left, right):
    return jnp.dot(left, right, preferred_element_type=f32)


def mm_t(left, right):
    return lax.dot_general(left, right, (((1,), (1,)), ((), ())), preferred_element_type=f32)


def stats_kernel(x_ref, o_ref):
    rows, _, lanes = x_ref.shape
    ones = jnp.ones((8, lanes), bf16)

    def body(row, carry):
        x = x_ref[row]
        wide = x.astype(f32)
        square = wide * wide
        high = square.astype(bf16)
        low = (square - high.astype(f32)).astype(bf16)
        o_ref[0, pl.ds(row, 1), :] = mm_t(ones, x)[0:1]
        o_ref[1, pl.ds(row, 1), :] = (mm_t(ones, high) + mm_t(ones, low))[0:1]
        return carry

    lax.fori_loop(0, rows, body, 0, unroll=2)


def add_kernel(left_ref, right_ref, o_ref):
    o_ref[...] = left_ref[...] + right_ref[...]


def warm_kernel(*refs):
    count = len(refs) // 2
    for source, target in zip(refs[:count], refs[count:]):
        target[...] = source[...]


def moments(left_ref, right_ref, channels):
    center = (left_ref[0] + right_ref[0]) / channels
    spread = (left_ref[1] + right_ref[1]) / channels - center * center
    return jnp.transpose(jnp.concatenate([center, lax.rsqrt(spread + norm_eps)], axis=0))


def normed_row(source, flipped, row, rows, gain):
    column = lax.broadcasted_iota(jnp.int32, flipped.shape, 1)
    center = jnp.sum(jnp.where(column == row, flipped, 0.0), axis=1, keepdims=True)
    factor = jnp.sum(jnp.where(column == row + rows, flipped, 0.0), axis=1, keepdims=True)
    return (source - center) * factor * gain


def forward_kernel(channels, scale, x_ref, left_ref, right_ref, gain_ref, table_ref, o_ref, f_ref):
    rows, _, lanes = x_ref.shape
    owners = o_ref.shape[0]
    f_ref[...] = moments(left_ref, right_ref, channels)

    def body(pair, carry):
        sides = [
            normed_row(x_ref[row].astype(f32), f_ref[...], row, rows, gain_ref[...]).astype(bf16)
            for row in (2 * pair, 2 * pair + 1)
        ]
        out = mm(table_ref[...], jnp.concatenate(sides, axis=1)) * scale
        for side in range(2):
            o_ref[:, 2 * pair + side] = (
                out[:, side * lanes : (side + 1) * lanes].reshape(owners, -1, lanes).astype(bf16)
            )
        return carry

    lax.fori_loop(0, rows // 2, body, 0)


def residual_kernel(channels, x_ref, left_ref, right_ref, gain_ref, o_ref, f_ref):
    rows = x_ref.shape[0]
    f_ref[...] = moments(left_ref, right_ref, channels)

    def body(row, carry):
        source = x_ref[row].astype(f32)
        o_ref[row] = normed_row(source, f_ref[...], row, rows, gain_ref[...]) + source
        return carry

    lax.fori_loop(0, rows, body, 0)


def flip_kernel(per_owner, lanes, table_ref, i_ref):
    for start in range(0, table_ref.shape[0], lanes):
        place = lax.broadcasted_iota(jnp.int32, (lanes, 1), 0) + start
        weight = jnp.where((place == 0) | (place == per_owner), 1.0, 2.0)
        part = table_ref[start : start + lanes, :].astype(f32) * weight
        i_ref[:, start : start + lanes] = jnp.transpose(part).astype(bf16)


def soften(values):
    return jnp.where(
        values > shrink_level,
        values - shrink_level,
        jnp.where(values < -shrink_level, values + shrink_level, 0.0),
    )


def block_matrix(w_ref, part):
    count, size = w_ref.shape[1], w_ref.shape[2]
    rows = []
    for block in range(count):
        cells = [jnp.zeros((size, size), f32)] * count
        cells[block] = w_ref[part, block]
        rows.append(jnp.concatenate(cells, axis=1))
    return jnp.concatenate(rows, axis=0)


def complex_matrix(w_ref):
    real, imag = block_matrix(w_ref, 0), block_matrix(w_ref, 1)
    return jnp.concatenate(
        [jnp.concatenate([real, imag], axis=1), jnp.concatenate([-imag, real], axis=1)], axis=0
    ).astype(bf16)


def bias_row(b_ref):
    parts, count = b_ref.shape[0], b_ref.shape[1]
    return jnp.concatenate(
        [b_ref[part, block : block + 1, :] for part in range(parts) for block in range(count)], axis=1
    )


def column_kernel(
    scale, x_ref, table_ref, w_ref, o_ref, wide_ref, real_ref, imag_ref
):
    size = w_ref.shape[1]
    tail = w_ref[2 * size :, :].astype(f32)
    bias_one, bias_two = tail[0:1] + tail[1:2], tail[2:3] + tail[3:4]
    height = table_ref.shape[1]
    lanes = x_ref.shape[1]
    step = x_ref.shape[0] // height
    count = step // 2
    wide_ref[...] = x_ref[...].astype(f32)
    for part, target in ((0, real_ref), (1, imag_ref)):
        for k in range(count):
            target[:, k * lanes : (k + 1) * lanes] = wide_ref[
                pl.ds(part * count + k, height, stride=step), :
            ].astype(bf16)

    def body(half, carry):
        span = pl.ds(pl.multiple_of(half * 2 * lanes, 2 * lanes), 2 * lanes)
        cos, sin = table_ref[0:height, :], table_ref[height:, :]
        real, imag = real_ref[:, span], imag_ref[:, span]
        out_real = (mm(cos, real) + mm(sin, imag)) * scale
        out_imag = (mm(cos, imag) - mm(sin, real)) * scale
        next_real, next_imag = [], []
        for side in range(2):
            cut = slice(side * lanes, (side + 1) * lanes)
            both = jnp.concatenate([out_real[:, cut].astype(bf16), out_imag[:, cut].astype(bf16)], axis=1)
            first = jnp.maximum(mm(both, w_ref[0:size, :]) + bias_one, 0.0).astype(bf16)
            second = soften(mm(first, w_ref[size : 2 * size, :]) + bias_two).astype(bf16)
            next_real.append(second[:, :lanes])
            next_imag.append(second[:, lanes:])
        real, imag = jnp.concatenate(next_real, axis=1), jnp.concatenate(next_imag, axis=1)
        back_real = (mm(cos, real) - mm(sin, imag)) * scale
        back_imag = (mm(cos, imag) + mm(sin, real)) * scale
        for side in range(2):
            cut = slice(side * lanes, (side + 1) * lanes)
            k = half * 2 + side
            wide_ref[pl.ds(k, height, stride=step), :] = back_real[:, cut]
            wide_ref[pl.ds(count + k, height, stride=step), :] = back_imag[:, cut]
        return carry

    lax.fori_loop(0, count // 2, body, 0)
    o_ref[...] = wide_ref[...].astype(bf16)


def inverse_kernel(scale, me_ref, x_ref, table_ref, r_ref, *refs):
    *o_refs, m_ref = refs
    ways = len(o_refs) // 2
    rows, _, lanes = r_ref.shape

    def body(pair, carry):
        sides = [
            x_ref[:, 2 * pair + side].astype(f32).reshape(-1, lanes).astype(bf16) for side in range(2)
        ]
        out = mm(table_ref[...], jnp.concatenate(sides, axis=1)) * scale
        for side in range(2):
            m_ref[side, pair] = (out[:, side * lanes : (side + 1) * lanes] + r_ref[2 * pair + side]).astype(bf16)
        return carry

    lax.fori_loop(0, rows // 2, body, 0)
    for shift in range(ways):
        for side in range(2):
            o_refs[side * ways + shift][...] = m_ref[side, lax.rem(me_ref[0] + shift, ways)]


def gelu(values):
    return 0.5 * values * (1.0 + lax.erf(values * math.sqrt(0.5)))


def mlp_kernel(
    tile, me_ref, x0, x1, x2, x3, wa_ref, wb_ref, gain_ref, bias_ref, y0, y1, y2, y3, x_ref, y_ref, n_ref, a_ref
):
    ways, tokens, lanes = x_ref.shape
    channels = ways * lanes
    me = me_ref[0]
    for shift, ref in enumerate((x0, x1, x2, x3)):
        x_ref[lax.rem(me + ways - shift, ways)] = ref[...]
    unit = jnp.ones((8, lanes), bf16)
    hidden_block = 512

    def body(index, carry):
        span = pl.ds(pl.multiple_of(index * tile, tile), tile)
        mixed = [x_ref[block, span, :].astype(f32) for block in range(ways)]
        total = sum(mixed[1:], mixed[0])
        square = sum((m * m for m in mixed[1:]), mixed[0] * mixed[0])
        center = jnp.sum(total, axis=1, keepdims=True) / channels
        spread = jnp.sum(square, axis=1, keepdims=True) / channels - center * center
        inverse = lax.rsqrt(spread + norm_eps)
        for b, m in enumerate(mixed):
            cut = slice(b * lanes, (b + 1) * lanes)
            n_ref[:, cut] = ((m - center) * inverse * gain_ref[:, cut]).astype(bf16)
            a_ref[:, cut] = m + bias_ref[b : b + 1, :]

        def block(place, inner):
            rows = pl.ds(pl.multiple_of(place * hidden_block, hidden_block), hidden_block)
            product = None
            for ref in (wa_ref, wb_ref):
                bias = mm_t(unit, ref[rows, 2 * channels :])[0:1]
                hidden = gelu(mm_t(n_ref[...], ref[rows, :channels]) + bias).astype(bf16)
                part = mm(hidden, ref[rows, channels : 2 * channels])
                product = part if product is None else product + part
            a_ref[...] += product
            return inner

        lax.fori_loop(0, wa_ref.shape[0] // hidden_block, block, 0)
        for b in range(ways):
            y_ref[b, span, :] = a_ref[:, b * lanes : (b + 1) * lanes].astype(bf16)
        return carry

    lax.fori_loop(0, tokens // tile, body, 0)
    for shift, ref in enumerate((y0, y1, y2, y3)):
        ref[...] = y_ref[lax.rem(me + shift, ways)]


def place_kernel(me_ref, *refs):
    *parts, o_ref = refs
    ways = o_ref.shape[0]
    half = o_ref.shape[1] // 2
    for place, part in enumerate(parts):
        shift = place % ways
        o_ref[lax.rem(me_ref[0] + ways - shift, ways), pl.ds(place // ways * half, half), :] = part[...]


def piece_kernel(
    piece_ref, one_ref, bias_ref, two_ref, out_ref, o_ref, flat_ref
):
    channels = one_ref.shape[0]
    lanes = o_ref.shape[1] - 2 * channels
    units = (o_ref.shape[0] - 16) // 2
    row = lax.broadcasted_iota(jnp.int32, (lanes, lanes), 0)
    column = lax.broadcasted_iota(jnp.int32, (lanes, lanes), 1)
    unit = jnp.where(row == column, 1.0, 0.0).astype(bf16)
    for half in range(2):
        first = half * (one_ref.shape[1] // 2) + piece_ref[half] * units
        slab = pl.ds(pl.multiple_of(first // lanes * lanes, lanes), lanes)
        bias = jnp.broadcast_to(bias_ref[:, slab].astype(f32), (lanes, lanes))
        flat_ref[:, 0:channels] = mm_t(unit, one_ref[:, slab])
        flat_ref[:, channels:] = jnp.where(row == column, bias, 0.0)
        within = pl.ds(pl.multiple_of(lax.rem(first, lanes), units), units)
        target = pl.ds(half * units, units)
        o_ref[target, 0:channels] = flat_ref[within, 0:channels].astype(bf16)
        o_ref[target, channels : 2 * channels] = two_ref[pl.ds(pl.multiple_of(first, units), units), :]
        o_ref[target, 2 * channels :] = flat_ref[within, channels:].astype(bf16)
    tail = pl.ds(2 * units, 16)
    o_ref[tail, :] = jnp.zeros((16, o_ref.shape[1]), bf16)
    o_ref[tail, 0:lanes] = jnp.broadcast_to(out_ref[...].astype(f32), (16, lanes)).astype(bf16)


def prep_kernel(w1_ref, b1_ref, w2_ref, b2_ref, o_ref):
    size = o_ref.shape[1]
    o_ref[0:size, :] = complex_matrix(w1_ref)
    o_ref[size : 2 * size, :] = complex_matrix(w2_ref)
    rows = []
    for ref in (b1_ref, b2_ref):
        bias = bias_row(ref)
        high = bias.astype(bf16).astype(f32)
        rows += [high, bias - high]
    rows.append(jnp.zeros((12, size), f32))
    o_ref[2 * size :, :] = jnp.concatenate(rows, axis=0).astype(bf16)


def split_kernel(me_ref, *refs):
    *parts, first_ref, second_ref, bias_ref = refs
    ways = len(parts)
    lanes = bias_ref.shape[1]
    size = first_ref.shape[0] // ways
    for place, part in enumerate(parts):
        for half, ref in enumerate((first_ref, second_ref)):
            ref[place * size : (place + 1) * size, :] = part[half * size : (half + 1) * size, :]
        row = part[2 * size : 2 * size + 16, 0:lanes].astype(f32)[0:1]
        bias_ref[pl.ds(lax.rem(me_ref[0] + ways - place, ways), 1), :] = row


def join_kernel(*refs):
    *parts, after_ref, o_ref = refs
    start = 0
    for part in parts:
        o_ref[start : start + part.shape[0], :] = part[...]
        start += part.shape[0]


def vmem(count):
    return [pl.BlockSpec(memory_space=pltpu.VMEM)] * count


smem = pl.BlockSpec(memory_space=pltpu.SMEM)


def call(kernel, shapes, in_specs, scratch=(), flops=0, size=0):
    return pl.pallas_call(
        kernel,
        out_shape=shapes,
        in_specs=in_specs,
        out_specs=jax.tree.map(lambda _: pl.BlockSpec(memory_space=pltpu.VMEM), shapes),
        scratch_shapes=scratch,
        cost_estimate=pl.CostEstimate(flops=flops, bytes_accessed=size, transcendentals=0),
        compiler_params=pltpu.CompilerParams(vmem_limit_bytes=24 * 1024 * 1024),
    )


def shape(dims, dtype):
    return jax.ShapeDtypeStruct(dims, dtype)


def shifts(value_of, axis, ways):
    return [
        lax.ppermute(value_of(shift), axis, [(i, (i + shift) % ways) for i in range(ways)])
        for shift in range(1, ways)
    ]


def local(
    tokens,
    gain_in,
    spectral_w1,
    spectral_b1,
    spectral_w2,
    spectral_b2,
    gain_out,
    fc1_weight,
    fc1_bias,
    fc2_weight,
    fc2_bias,
):
    rows, width, lanes = tokens.shape
    ways = lax.axis_size("chan")
    owners = lax.axis_size("rows")
    height = rows * owners
    channels = lanes * ways
    per_owner = width // 2 // owners
    me = lax.axis_index("chan").astype(jnp.int32).reshape(1)
    forward, cos, sin = tables(height, width, per_owner)
    forward = jnp.asarray(forward, bf16)
    turns = jnp.asarray(np.concatenate([cos, sin], axis=0), bf16)
    half_scale = 2.0 ** math.floor(math.log2(math.sqrt(width)))
    first_scale, second_scale = 1.0 / half_scale, half_scale / math.sqrt(width * height)

    stats = call(stats_kernel, shape((2, rows, width), f32), vmem(1))(tokens)
    other = lax.ppermute(stats, "chan", [(i, i ^ 1) for i in range(ways)])
    left = call(add_kernel, shape(stats.shape, f32), vmem(2))(stats, other)
    right = lax.ppermute(left, "chan", [(i, i ^ 2) for i in range(ways)])
    table, gain = call(
        warm_kernel, [shape(forward.shape, bf16), shape((1, lanes), f32)], vmem(2)
    )(forward, gain_in.reshape(1, lanes))
    spectra = call(
        partial(forward_kernel, channels, first_scale),
        shape((owners, rows, 2 * per_owner, lanes), bf16),
        vmem(5),
        scratch=[pltpu.VMEM((width, 2 * rows), f32)],
    )(tokens, left, right, gain, table)
    columns = lax.all_to_all(spectra, "rows", split_axis=0, concat_axis=0)

    ring_x, ring_y, per_x = 4, 4, owners // 4
    place = lax.axis_index("rows").astype(jnp.int32)
    units = fc1_weight.shape[1] // (2 * ring_x)
    across, along, core = place // per_x, place // 2 % ring_y, place % 2
    piece = jnp.stack([across * 2 + core, along * 2 + core])
    mine = call(
        piece_kernel,
        shape((units + 16, 2 * channels + lanes), bf16),
        [smem] + vmem(4),
        scratch=[pltpu.VMEM((lanes, channels + lanes), f32)],
    )(piece, fc1_weight, fc1_bias.reshape(1, -1), fc2_weight, fc2_bias.reshape(1, lanes))
    wide = 2 * lanes
    spectral = call(prep_kernel, shape((2 * wide + 16, wide), bf16), vmem(4))(
        spectral_w1, spectral_b1, spectral_w2, spectral_b2
    )
    circle = call(warm_kernel, [shape(turns.shape, bf16)], vmem(1))(turns)[0]
    stage = [mine] + shifts(lambda s: mine, "chan", ways)
    count = ways * units // 2
    *sides, out_bias = call(
        split_kernel,
        [shape((count, mine.shape[1]), bf16)] * 2 + [shape((8, lanes), f32)],
        [smem] + vmem(ways),
    )(me, *stage)
    parts = list(sides)
    for shift in range(1, ring_x):
        ring = [
            [(i, (i + shift * per_x) % owners) for i in range(owners)],
            [(i, i + 2 * ((i // 2 % ring_y + shift) % ring_y - i // 2 % ring_y)) for i in range(owners)],
        ]
        for half in range(2):
            parts.append(lax.ppermute(sides[half], "rows", ring[half]))

    total = owners * rows * 2 * per_owner
    back = call(
        partial(column_kernel, second_scale),
        shape((total, lanes), bf16),
        vmem(3),
        scratch=[
            pltpu.VMEM((total, lanes), f32),
            pltpu.VMEM((height, per_owner * lanes), bf16),
            pltpu.VMEM((height, per_owner * lanes), bf16),
        ],
    )(columns.reshape(total, lanes), circle, spectral)
    returned = lax.all_to_all(
        back.reshape(owners, rows, 2 * per_owner, lanes), "rows", split_axis=0, concat_axis=0
    )
    resid = call(
        partial(residual_kernel, channels),
        shape((rows, width, lanes), f32),
        vmem(4),
        scratch=[pltpu.VMEM((width, 2 * rows), f32)],
    )(tokens, left, right, gain_in.reshape(1, lanes))
    inverse = call(partial(flip_kernel, per_owner, lanes), shape((width, width), bf16), vmem(1))(forward)
    share = rows // ways * width // 2
    mixed = call(
        partial(inverse_kernel, first_scale),
        [shape((share, lanes), bf16)] * (2 * ways),
        [smem] + vmem(3),
        scratch=[pltpu.VMEM((2, ways, width, lanes), bf16)],
    )(me, returned, inverse, resid)
    halves = [mixed[:ways], mixed[ways:]]
    whole_a = [halves[0][0]] + shifts(lambda s: halves[0][s], "chan", ways)
    near = call(
        join_kernel,
        shape((2 * ring_x * parts[0].shape[0], parts[0].shape[1]), bf16),
        vmem(len(parts)) + [pl.BlockSpec(memory_space=pl.ANY)],
    )(*parts, mixed[0])
    far = lax.ppermute(near, "rows", [(i, i ^ 1) for i in range(owners)])
    whole_b = [halves[1][0]] + shifts(lambda s: halves[1][s], "chan", ways)

    def mlp(whole):
        return call(
            partial(mlp_kernel, 256),
            [shape((share, lanes), bf16)] * ways,
            [smem] + vmem(8),
            scratch=[
                pltpu.VMEM((ways, share, lanes), bf16),
                pltpu.VMEM((ways, share, lanes), bf16),
                pltpu.VMEM((256, channels), bf16),
                pltpu.VMEM((256, channels), f32),
            ],
        )(me, *whole, near, far, gain_out.reshape(1, channels), out_bias)

    result_a = mlp(whole_a)
    parts_a = [result_a[0]] + shifts(lambda s: result_a[s], "chan", ways)
    result_b = mlp(whole_b)
    parts_b = [result_b[0]] + shifts(lambda s: result_b[s], "chan", ways)
    final = call(place_kernel, shape((ways, 2 * share, lanes), bf16), [smem] + vmem(2 * ways))(
        me, *parts_a, *parts_b
    )
    return final.reshape(rows, width, lanes)


def solution(mesh):
    return jax.shard_map(
        local,
        mesh=mesh,
        in_specs=(
            P("rows", None, "chan"),
            P("chan"),
            P(None, "chan", None, None),
            P(None, "chan", None),
            P(None, "chan", None, None),
            P(None, "chan", None),
            P(),
            P(None, "chan"),
            P("chan"),
            P("chan", None),
            P("chan"),
        ),
        out_specs=P("rows", None, "chan"),
        check_vma=False,
    )
```

```python
import math
from functools import partial

import jax
import jax.numpy as jnp
import numpy as np
from jax import lax
from jax.experimental import pallas as pl
from jax.experimental.pallas import tpu as pltpu
from jax.sharding import PartitionSpec as P

norm_eps = 1e-05
shrink_level = 0.01
bf16 = jnp.bfloat16
f32 = jnp.float32


def tables(rows, width, per_owner):
    owners = width // 2 // per_owner
    place = np.arange(width)
    freq = np.arange(width // 2).reshape(owners, 1, per_owner)
    freq = np.broadcast_to(freq, (owners, 2, per_owner)).reshape(-1)
    part = np.broadcast_to(np.arange(2).reshape(1, 2, 1), (owners, 2, per_owner)).reshape(-1)
    angle = 2.0 * np.pi / width * ((freq[:, None] * place[None, :]) % width)
    forward = np.where(part[:, None] == 0, np.cos(angle), -np.sin(angle))
    grid = np.arange(rows)
    turn = 2.0 * np.pi / rows * ((grid[:, None] * grid[None, :]) % rows)
    return forward, np.cos(turn), np.sin(turn)


def mm(left, right):
    return jnp.dot(left, right, preferred_element_type=f32)


def mm_t(left, right):
    return lax.dot_general(left, right, (((1,), (1,)), ((), ())), preferred_element_type=f32)


def stats_kernel(x_ref, o_ref):
    rows, _, lanes = x_ref.shape
    ones = jnp.ones((8, lanes), bf16)

    for row in range(rows):
        x = x_ref[row]
        wide = x.astype(f32)
        square = wide * wide
        high = square.astype(bf16)
        low = (square - high.astype(f32)).astype(bf16)
        o_ref[0, row : row + 1, :] = mm_t(ones, x)[0:1]
        o_ref[1, row : row + 1, :] = (mm_t(ones, high) + mm_t(ones, low))[0:1]


def add_kernel(left_ref, right_ref, o_ref):
    o_ref[...] = left_ref[...] + right_ref[...]


def warm_kernel(*refs):
    count = len(refs) // 2
    for source, target in zip(refs[:count], refs[count:]):
        target[...] = source[...]


def moments(left_ref, right_ref, channels):
    center = (left_ref[0] + right_ref[0]) / channels
    spread = (left_ref[1] + right_ref[1]) / channels - center * center
    return jnp.transpose(jnp.concatenate([center, lax.rsqrt(spread + norm_eps)], axis=0))


def normed_row(source, flipped, row, rows, gain):
    return (source - flipped[:, row : row + 1]) * flipped[:, rows + row : rows + row + 1] * gain


def forward_kernel(channels, scale, x_ref, left_ref, right_ref, gain_ref, table_ref, o_ref):
    rows, _, lanes = x_ref.shape
    owners = o_ref.shape[0]
    flipped = moments(left_ref, right_ref, channels)
    gain = gain_ref[...]
    for pair in range(rows // 2):
        sides = [
            normed_row(x_ref[row].astype(f32), flipped, row, rows, gain).astype(bf16)
            for row in (2 * pair, 2 * pair + 1)
        ]
        out = mm(table_ref[...], jnp.concatenate(sides, axis=1)) * scale
        for side in range(2):
            o_ref[:, 2 * pair + side] = (
                out[:, side * lanes : (side + 1) * lanes].reshape(owners, -1, lanes).astype(bf16)
            )


def residual_kernel(channels, x_ref, left_ref, right_ref, gain_ref, o_ref):
    rows = x_ref.shape[0]
    flipped = moments(left_ref, right_ref, channels)
    for row in range(rows):
        source = x_ref[row].astype(f32)
        o_ref[row] = normed_row(source, flipped, row, rows, gain_ref[...]) + source


def flip_kernel(per_owner, lanes, table_ref, i_ref):
    for start in range(0, table_ref.shape[0], lanes):
        place = lax.broadcasted_iota(jnp.int32, (lanes, 1), 0) + start
        weight = jnp.where((place == 0) | (place == per_owner), 1.0, 2.0)
        part = table_ref[start : start + lanes, :].astype(f32) * weight
        i_ref[:, start : start + lanes] = jnp.transpose(part).astype(bf16)


def soften(values):
    return jnp.where(
        values > shrink_level,
        values - shrink_level,
        jnp.where(values < -shrink_level, values + shrink_level, 0.0),
    )


def block_matrix(w_ref, part):
    count, size = w_ref.shape[1], w_ref.shape[2]
    rows = []
    for block in range(count):
        cells = [jnp.zeros((size, size), f32)] * count
        cells[block] = w_ref[part, block]
        rows.append(jnp.concatenate(cells, axis=1))
    return jnp.concatenate(rows, axis=0)


def complex_matrix(w_ref):
    real, imag = block_matrix(w_ref, 0), block_matrix(w_ref, 1)
    return jnp.concatenate(
        [jnp.concatenate([real, imag], axis=1), jnp.concatenate([-imag, real], axis=1)], axis=0
    ).astype(bf16)


def bias_row(b_ref):
    parts, count = b_ref.shape[0], b_ref.shape[1]
    return jnp.concatenate(
        [b_ref[part, block : block + 1, :] for part in range(parts) for block in range(count)], axis=1
    )


def column_kernel(
    scale, x_ref, table_ref, w_ref, o_ref, wide_ref, real_ref, imag_ref
):
    size = w_ref.shape[1]
    tail = w_ref[2 * size :, :].astype(f32)
    bias_one, bias_two = tail[0:1] + tail[1:2], tail[2:3] + tail[3:4]
    height = table_ref.shape[1]
    lanes = x_ref.shape[1]
    step = x_ref.shape[0] // height
    count = step // 2
    wide_ref[...] = x_ref[...].astype(f32)
    for part, target in ((0, real_ref), (1, imag_ref)):
        for k in range(count):
            target[:, k * lanes : (k + 1) * lanes] = wide_ref[
                pl.ds(part * count + k, height, stride=step), :
            ].astype(bf16)

    for half in range(count // 2):
        span = pl.ds(half * 2 * lanes, 2 * lanes)
        cos, sin = table_ref[0:height, :], table_ref[height:, :]
        real, imag = real_ref[:, span], imag_ref[:, span]
        out_real = (mm(cos, real) + mm(sin, imag)) * scale
        out_imag = (mm(cos, imag) - mm(sin, real)) * scale
        next_real, next_imag = [], []
        for side in range(2):
            cut = slice(side * lanes, (side + 1) * lanes)
            both = jnp.concatenate([out_real[:, cut].astype(bf16), out_imag[:, cut].astype(bf16)], axis=1)
            first = jnp.maximum(mm(both, w_ref[0:size, :]) + bias_one, 0.0).astype(bf16)
            second = soften(mm(first, w_ref[size : 2 * size, :]) + bias_two).astype(bf16)
            next_real.append(second[:, :lanes])
            next_imag.append(second[:, lanes:])
        real, imag = jnp.concatenate(next_real, axis=1), jnp.concatenate(next_imag, axis=1)
        back_real = (mm(cos, real) - mm(sin, imag)) * scale
        back_imag = (mm(cos, imag) + mm(sin, real)) * scale
        for side in range(2):
            cut = slice(side * lanes, (side + 1) * lanes)
            k = half * 2 + side
            wide_ref[pl.ds(k, height, stride=step), :] = back_real[:, cut]
            wide_ref[pl.ds(count + k, height, stride=step), :] = back_imag[:, cut]
    o_ref[...] = wide_ref[...].astype(bf16)


def inverse_kernel(scale, me_ref, x_ref, table_ref, r_ref, *o_refs):
    ways = len(o_refs) // 2
    _, _, lanes = r_ref.shape
    for shift in range(ways):
        owner = lax.rem(me_ref[0] + shift, ways)
        sides = [
            x_ref[:, 2 * owner + side].astype(f32).reshape(-1, lanes).astype(bf16) for side in range(2)
        ]
        out = mm(table_ref[...], jnp.concatenate(sides, axis=1)) * scale
        for side in range(2):
            o_refs[side * ways + shift][...] = (
                out[:, side * lanes : (side + 1) * lanes] + r_ref[2 * owner + side]
            ).astype(bf16)


def gelu(values):
    return 0.5 * values * (1.0 + lax.erf(values * math.sqrt(0.5)))


def eye(rows, columns):
    row = lax.broadcasted_iota(jnp.int32, (rows, columns), 0)
    column = lax.broadcasted_iota(jnp.int32, (rows, columns), 1)
    return jnp.where(row == column, 1.0, 0.0)


def mlp_kernel(
    tile, me_ref, x0, x1, x2, x3, wa_ref, wb_ref, gain_ref, bias_ref, y0, y1, y2, y3, x_ref, y_ref
):
    ways, tokens, lanes = x_ref.shape
    channels = ways * lanes
    me = me_ref[0]
    for shift, ref in enumerate((x0, x1, x2, x3)):
        x_ref[lax.rem(me + ways - shift, ways)] = ref[...]
    unit = eye(8, lanes).astype(bf16)
    hidden_block = 512
    blocks = [
        (ref, pl.ds(start, hidden_block))
        for ref in (wa_ref, wb_ref)
        for start in range(0, ref.shape[0], hidden_block)
    ]
    biases = [mm_t(unit, ref[span, 2 * channels :])[0:1] for ref, span in blocks]

    def body(index, carry):
        span = pl.ds(pl.multiple_of(index * tile, tile), tile)
        mixed = [x_ref[block, span, :].astype(f32) for block in range(ways)]
        total = sum(mixed[1:], mixed[0])
        square = sum((m * m for m in mixed[1:]), mixed[0] * mixed[0])
        center = jnp.sum(total, axis=1, keepdims=True) / channels
        spread = jnp.sum(square, axis=1, keepdims=True) / channels - center * center
        inverse = lax.rsqrt(spread + norm_eps)
        normed = jnp.concatenate(
            [
                ((m - center) * inverse * gain_ref[:, b * lanes : (b + 1) * lanes]).astype(bf16)
                for b, m in enumerate(mixed)
            ],
            axis=1,
        )
        acc = None
        for (ref, rows), bias in zip(blocks, biases):
            hidden = gelu(mm_t(normed, ref[rows, :channels]) + bias).astype(bf16)
            product = mm(hidden, ref[rows, channels : 2 * channels])
            acc = product if acc is None else acc + product
        for b in range(ways):
            cut = slice(b * lanes, (b + 1) * lanes)
            y_ref[b, span, :] = (mixed[b] + acc[:, cut] + bias_ref[b : b + 1, :]).astype(bf16)
        return carry

    lax.fori_loop(0, tokens // tile, body, 0)
    for shift, ref in enumerate((y0, y1, y2, y3)):
        ref[...] = y_ref[lax.rem(me + shift, ways)]


def place_kernel(me_ref, *refs):
    *parts, o_ref = refs
    ways = o_ref.shape[0]
    half = o_ref.shape[1] // 2
    for place, part in enumerate(parts):
        shift = place % ways
        o_ref[lax.rem(me_ref[0] + ways - shift, ways), pl.ds(place // ways * half, half), :] = part[...]


def piece_kernel(piece_ref, one_ref, bias_ref, two_ref, out_ref, o_ref, flat_ref):
    channels = one_ref.shape[0]
    lanes = o_ref.shape[1] - 2 * channels
    units = o_ref.shape[0] // 2
    square = eye(lanes, lanes)
    place = lax.broadcasted_iota(jnp.int32, (units, lanes), 1)
    extra = jnp.sum(square * out_ref[...].astype(f32), axis=1, keepdims=True)
    for half in range(2):
        first = half * (one_ref.shape[1] // 2) + piece_ref[half] * units
        slab = pl.ds(pl.multiple_of(first // lanes * lanes, lanes), lanes)
        flat_ref[:, 0:channels] = mm_t(square.astype(bf16), one_ref[:, slab])
        flat_ref[:, channels:] = square * bias_ref[:, slab].astype(f32)
        within = pl.ds(pl.multiple_of(lax.rem(first, lanes), units), units)
        target = pl.ds(half * units, units)
        o_ref[target, 0:channels] = flat_ref[within, 0:channels].astype(bf16)
        o_ref[target, channels : 2 * channels] = two_ref[pl.ds(pl.multiple_of(first, units), units), :]
        bias = jnp.sum(flat_ref[within, channels:], axis=1, keepdims=True)
        near = extra[half * units : (half + 1) * units]
        far = extra[(2 + half) * units : (3 + half) * units]
        values = jnp.where(place == 0, bias, jnp.where(place == 1, near, jnp.where(place == 2, far, 0.0)))
        o_ref[target, 2 * channels :] = values.astype(bf16)


def prep_kernel(w1_ref, b1_ref, w2_ref, b2_ref, o_ref):
    size = o_ref.shape[1]
    o_ref[0:size, :] = complex_matrix(w1_ref)
    o_ref[size : 2 * size, :] = complex_matrix(w2_ref)
    rows = []
    for ref in (b1_ref, b2_ref):
        bias = bias_row(ref)
        high = bias.astype(bf16).astype(f32)
        rows += [high, bias - high]
    rows.append(jnp.zeros((12, size), f32))
    o_ref[2 * size :, :] = jnp.concatenate(rows, axis=0).astype(bf16)


def split_kernel(me_ref, *refs):
    *parts, first_ref, second_ref, bias_ref = refs
    ways = len(parts)
    lanes = bias_ref.shape[1]
    size = first_ref.shape[0] // ways
    for place, part in enumerate(parts):
        for half, ref in enumerate((first_ref, second_ref)):
            ref[place * size : (place + 1) * size, :] = part[half * size : (half + 1) * size, :]
        found = mm_t(eye(8, lanes).astype(bf16), part[:, part.shape[1] - lanes :])
        row = jnp.concatenate([found[1:2], found[2:3]], axis=1)
        bias_ref[pl.ds(lax.rem(me_ref[0] + ways - place, ways), 1), :] = row


def join_kernel(*refs):
    *parts, o_ref = refs
    start = 0
    for part in parts:
        o_ref[start : start + part.shape[0], :] = part[...]
        start += part.shape[0]


def vmem(count):
    return [pl.BlockSpec(memory_space=pltpu.VMEM)] * count


smem = pl.BlockSpec(memory_space=pltpu.SMEM)


def call(kernel, shapes, in_specs, scratch=(), flops=0, size=0):
    return pl.pallas_call(
        kernel,
        out_shape=shapes,
        in_specs=in_specs,
        out_specs=jax.tree.map(lambda _: pl.BlockSpec(memory_space=pltpu.VMEM), shapes),
        scratch_shapes=scratch,
        cost_estimate=pl.CostEstimate(flops=flops, bytes_accessed=size, transcendentals=0),
        compiler_params=pltpu.CompilerParams(vmem_limit_bytes=24 * 1024 * 1024),
    )


def shape(dims, dtype):
    return jax.ShapeDtypeStruct(dims, dtype)


def shifts(value_of, axis, ways):
    return [
        lax.ppermute(value_of(shift), axis, [(i, (i + shift) % ways) for i in range(ways)])
        for shift in range(1, ways)
    ]


def local(
    tokens,
    gain_in,
    spectral_w1,
    spectral_b1,
    spectral_w2,
    spectral_b2,
    gain_out,
    fc1_weight,
    fc1_bias,
    fc2_weight,
    fc2_bias,
):
    rows, width, lanes = tokens.shape
    ways = lax.axis_size("chan")
    owners = lax.axis_size("rows")
    height = rows * owners
    channels = lanes * ways
    per_owner = width // 2 // owners
    me = lax.axis_index("chan").astype(jnp.int32).reshape(1)
    forward, cos, sin = tables(height, width, per_owner)
    forward = jnp.asarray(forward, bf16)
    turns = jnp.asarray(np.concatenate([cos, sin], axis=0), bf16)
    half_scale = 2.0 ** math.floor(math.log2(math.sqrt(width)))
    first_scale, second_scale = 1.0 / half_scale, half_scale / math.sqrt(width * height)

    stats = call(stats_kernel, shape((2, rows, width), f32), vmem(1))(tokens)
    other = lax.ppermute(stats, "chan", [(i, i ^ 1) for i in range(ways)])
    left = call(add_kernel, shape(stats.shape, f32), vmem(2))(stats, other)
    right = lax.ppermute(left, "chan", [(i, i ^ 2) for i in range(ways)])
    table, gain = call(
        warm_kernel, [shape(forward.shape, bf16), shape((1, lanes), f32)], vmem(2)
    )(forward, gain_in.reshape(1, lanes))
    spectra = call(
        partial(forward_kernel, channels, first_scale),
        shape((owners, rows, 2 * per_owner, lanes), bf16),
        vmem(5),
    )(tokens, left, right, gain, table)
    columns = lax.all_to_all(spectra, "rows", split_axis=0, concat_axis=0)

    ring_x, ring_y, per_x = 4, 4, owners // 4
    place = lax.axis_index("rows").astype(jnp.int32)
    units = fc1_weight.shape[1] // (2 * ring_x)
    across, along, core = place // per_x, place // 2 % ring_y, place % 2
    piece = jnp.stack([across * 2 + core, along * 2 + core])
    mine = call(
        piece_kernel,
        shape((units, 2 * channels + lanes), bf16),
        [smem] + vmem(4),
        scratch=[pltpu.VMEM((lanes, channels + lanes), f32)],
    )(piece, fc1_weight, fc1_bias.reshape(1, -1), fc2_weight, fc2_bias.reshape(1, lanes))
    wide = 2 * lanes
    spectral = call(prep_kernel, shape((2 * wide + 16, wide), bf16), vmem(4))(
        spectral_w1, spectral_b1, spectral_w2, spectral_b2
    )
    circle = call(warm_kernel, [shape(turns.shape, bf16)], vmem(1))(turns)[0]
    stage = [mine] + shifts(lambda s: mine, "chan", ways)
    count = ways * units // 2
    *sides, out_bias = call(
        split_kernel,
        [shape((count, mine.shape[1]), bf16)] * 2 + [shape((8, lanes), f32)],
        [smem] + vmem(ways),
    )(me, *stage)
    parts = list(sides)
    for shift in range(1, ring_x):
        ring = [
            [(i, (i + shift * per_x) % owners) for i in range(owners)],
            [(i, i + 2 * ((i // 2 % ring_y + shift) % ring_y - i // 2 % ring_y)) for i in range(owners)],
        ]
        for half in range(2):
            parts.append(lax.ppermute(sides[half], "rows", ring[half]))

    total = owners * rows * 2 * per_owner
    back = call(
        partial(column_kernel, second_scale),
        shape((total, lanes), bf16),
        vmem(3),
        scratch=[
            pltpu.VMEM((total, lanes), f32),
            pltpu.VMEM((height, per_owner * lanes), bf16),
            pltpu.VMEM((height, per_owner * lanes), bf16),
        ],
    )(columns.reshape(total, lanes), circle, spectral)
    returned = lax.all_to_all(
        back.reshape(owners, rows, 2 * per_owner, lanes), "rows", split_axis=0, concat_axis=0
    )
    resid = call(
        partial(residual_kernel, channels),
        shape((rows, width, lanes), f32),
        vmem(4),
    )(tokens, left, right, gain_in.reshape(1, lanes))
    inverse = call(partial(flip_kernel, per_owner, lanes), shape((width, width), bf16), vmem(1))(forward)
    share = rows // ways * width // 2
    mixed = call(
        partial(inverse_kernel, first_scale),
        [shape((share, lanes), bf16)] * (2 * ways),
        [smem] + vmem(3),
    )(me, returned, inverse, resid)
    halves = [mixed[:ways], mixed[ways:]]
    whole_a = [halves[0][0]] + shifts(lambda s: halves[0][s], "chan", ways)
    near = call(
        join_kernel,
        shape((2 * ring_x * parts[0].shape[0], parts[0].shape[1]), bf16),
        vmem(len(parts)),
    )(*parts)
    far = lax.ppermute(near, "rows", [(i, i ^ 1) for i in range(owners)])
    whole_b = [halves[1][0]] + shifts(lambda s: halves[1][s], "chan", ways)

    def mlp(whole):
        return call(
            partial(mlp_kernel, 256),
            [shape((share, lanes), bf16)] * ways,
            [smem] + vmem(8),
            scratch=[
                pltpu.VMEM((ways, share, lanes), bf16),
                pltpu.VMEM((ways, share, lanes), bf16),
            ],
        )(me, *whole, near, far, gain_out.reshape(1, channels), out_bias)

    result_a = mlp(whole_a)
    parts_a = [result_a[0]] + shifts(lambda s: result_a[s], "chan", ways)
    result_b = mlp(whole_b)
    parts_b = [result_b[0]] + shifts(lambda s: result_b[s], "chan", ways)
    final = call(place_kernel, shape((ways, 2 * share, lanes), bf16), [smem] + vmem(2 * ways))(
        me, *parts_a, *parts_b
    )
    return final.reshape(rows, width, lanes)


def solution(mesh):
    return jax.shard_map(
        local,
        mesh=mesh,
        in_specs=(
            P("rows", None, "chan"),
            P("chan"),
            P(None, "chan", None, None),
            P(None, "chan", None),
            P(None, "chan", None, None),
            P(None, "chan", None),
            P(),
            P(None, "chan"),
            P("chan"),
            P("chan", None),
            P("chan"),
        ),
        out_specs=P("rows", None, "chan"),
        check_vma=False,
    )
```

```python
import math
from functools import partial

import jax
import jax.numpy as jnp
import numpy as np
from jax import lax
from jax.experimental import pallas as pl
from jax.experimental.pallas import tpu as pltpu
from jax.sharding import PartitionSpec as P

norm_eps = 1e-05
shrink_level = 0.01
bf16 = jnp.bfloat16
f32 = jnp.float32


def circle_table(size):
    grid = np.arange(size)
    turn = 2.0 * np.pi / size * ((grid[:, None] * grid[None, :]) % size)
    return np.concatenate([np.cos(turn[: size // 2]), np.sin(turn[: size // 2])], axis=0)


def mm(left, right):
    return jnp.dot(left, right, preferred_element_type=f32)


def mm_t(left, right):
    return lax.dot_general(left, right, (((1,), (1,)), ((), ())), preferred_element_type=f32)


def stats_kernel(x_ref, o_ref):
    rows, _, lanes = x_ref.shape
    ones = jnp.ones((8, lanes), bf16)

    for row in range(rows):
        x = x_ref[row]
        wide = x.astype(f32)
        square = wide * wide
        high = square.astype(bf16)
        low = (square - high.astype(f32)).astype(bf16)
        o_ref[0, row : row + 1, :] = mm_t(ones, x)[0:1]
        o_ref[1, row : row + 1, :] = (mm_t(ones, high) + mm_t(ones, low))[0:1]


def add_kernel(left_ref, right_ref, o_ref):
    o_ref[...] = left_ref[...] + right_ref[...]


def table_kernel(per_owner, turn_ref, gain_ref, o_ref, g_ref, half_ref, full_ref):
    g_ref[...] = gain_ref[...]
    size, lanes = half_ref.shape
    owners = size // per_owner
    for lane in range(0, o_ref.shape[1], lanes):
        for part in range(2):
            start = part * (turn_ref.shape[0] // 2)
            half_ref[...] = turn_ref[start : start + size, lane : lane + lanes].astype(f32) * (1.0 - 2.0 * part)
            for place in range(per_owner):
                full_ref[pl.ds(part * per_owner + place, owners, stride=2 * per_owner), :] = half_ref[
                    pl.ds(place, owners, stride=per_owner), :
                ]
        o_ref[:, lane : lane + lanes] = full_ref[...].astype(bf16)


def turn_kernel(half_ref, w1_ref, b1_ref, w2_ref, b2_ref, o_ref):
    size, width = half_ref.shape[0] // 2, half_ref.shape[1]
    column = lax.broadcasted_iota(jnp.int32, (size, width), 1)
    sign = jnp.where(column % 2 == 0, 1.0, -1.0)
    for part in range(2):
        top = half_ref[part * size : (part + 1) * size, :]
        o_ref[2 * part * size : (2 * part + 1) * size, :] = top
        o_ref[(2 * part + 1) * size : (2 * part + 2) * size, :] = (top.astype(f32) * sign).astype(bf16)
    start, wide = 4 * size, o_ref.shape[1] // 2
    for place, (w_ref, b_ref) in enumerate(((w1_ref, b1_ref), (w2_ref, b2_ref))):
        cut = slice(place * wide, (place + 1) * wide)
        o_ref[start : start + wide, cut] = complex_matrix(w_ref)
        bias = bias_row(b_ref)
        high = bias.astype(bf16).astype(f32)
        rows = jnp.concatenate([high, bias - high, jnp.zeros((14, wide), f32)], axis=0)
        o_ref[start + wide :, cut] = rows.astype(bf16)


def moments(left_ref, right_ref, channels):
    center = (left_ref[0] + right_ref[0]) / channels
    spread = (left_ref[1] + right_ref[1]) / channels - center * center
    return jnp.transpose(jnp.concatenate([center, lax.rsqrt(spread + norm_eps)], axis=0))


def normed_row(source, flipped, row, rows, gain):
    return (source - flipped[:, row : row + 1]) * flipped[:, rows + row : rows + row + 1] * gain


def forward_kernel(channels, scale, x_ref, left_ref, right_ref, gain_ref, table_ref, o_ref):
    rows, _, lanes = x_ref.shape
    owners = o_ref.shape[0]
    flipped = moments(left_ref, right_ref, channels)
    gain = gain_ref[...]
    for pair in range(rows // 2):
        sides = [
            normed_row(x_ref[row].astype(f32), flipped, row, rows, gain).astype(bf16)
            for row in (2 * pair, 2 * pair + 1)
        ]
        out = mm(table_ref[...], jnp.concatenate(sides, axis=1)) * scale
        for side in range(2):
            o_ref[:, 2 * pair + side] = (
                out[:, side * lanes : (side + 1) * lanes].reshape(owners, -1, lanes).astype(bf16)
            )


def flip_kernel(per_owner, lanes, channels, table_ref, left_ref, right_ref, i_ref):
    for start in range(0, table_ref.shape[0], lanes):
        place = lax.broadcasted_iota(jnp.int32, (lanes, 1), 0) + start
        weight = jnp.where((place == 0) | (place == per_owner), 1.0, 2.0)
        part = table_ref[start : start + lanes, :].astype(f32) * weight
        i_ref[:, start : start + lanes] = jnp.transpose(part).astype(bf16)
    rest = moments(left_ref, right_ref, channels)
    pieces = []
    for _ in range(3):
        piece = rest.astype(bf16).astype(f32)
        pieces.append(piece)
        rest = rest - piece
    width, count = rest.shape
    pieces.append(jnp.zeros((width, lanes - 3 * count), f32))
    i_ref[:, table_ref.shape[0] :] = jnp.concatenate(pieces, axis=1).astype(bf16)


def soften(values):
    return jnp.where(
        values > shrink_level,
        values - shrink_level,
        jnp.where(values < -shrink_level, values + shrink_level, 0.0),
    )


def block_matrix(w_ref, part):
    count, size = w_ref.shape[1], w_ref.shape[2]
    rows = []
    for block in range(count):
        cells = [jnp.zeros((size, size), f32)] * count
        cells[block] = w_ref[part, block]
        rows.append(jnp.concatenate(cells, axis=1))
    return jnp.concatenate(rows, axis=0)


def complex_matrix(w_ref):
    real, imag = block_matrix(w_ref, 0), block_matrix(w_ref, 1)
    return jnp.concatenate(
        [jnp.concatenate([real, imag], axis=1), jnp.concatenate([-imag, real], axis=1)], axis=0
    ).astype(bf16)


def bias_row(b_ref):
    parts, count = b_ref.shape[0], b_ref.shape[1]
    return jnp.concatenate(
        [b_ref[part, block : block + 1, :] for part in range(parts) for block in range(count)], axis=1
    )


def column_kernel(
    scale, x_ref, table_ref, o_ref, wide_ref, real_ref, imag_ref
):
    size = 2 * x_ref.shape[1]
    start = 2 * table_ref.shape[1]
    tail = table_ref[start + size :, :].astype(f32)
    bias = tail[0:1] + tail[1:2]
    height = table_ref.shape[1]
    lanes = x_ref.shape[1]
    step = x_ref.shape[0] // height
    count = step // 2
    wide_ref[...] = x_ref[...].astype(f32)
    for part, target in ((0, real_ref), (1, imag_ref)):
        for k in range(count):
            target[:, k * lanes : (k + 1) * lanes] = wide_ref[
                pl.ds(part * count + k, height, stride=step), :
            ].astype(bf16)

    def body(half, carry):
        span = pl.ds(pl.multiple_of(half * 2 * lanes, 2 * lanes), 2 * lanes)
        cos, sin = table_ref[0:height, :], table_ref[height : 2 * height, :]
        real, imag = real_ref[:, span], imag_ref[:, span]
        out_real = (mm(cos, real) + mm(sin, imag)) * scale
        out_imag = (mm(cos, imag) - mm(sin, real)) * scale
        next_real, next_imag = [], []
        for side in range(2):
            cut = slice(side * lanes, (side + 1) * lanes)
            both = jnp.concatenate([out_real[:, cut].astype(bf16), out_imag[:, cut].astype(bf16)], axis=1)
            first = jnp.maximum(mm(both, table_ref[start : start + size, 0:size]) + bias[:, 0:size], 0.0).astype(bf16)
            second = soften(mm(first, table_ref[start : start + size, size:]) + bias[:, size:]).astype(bf16)
            next_real.append(second[:, :lanes])
            next_imag.append(second[:, lanes:])
        real, imag = jnp.concatenate(next_real, axis=1), jnp.concatenate(next_imag, axis=1)
        back_real = (mm(cos, real) - mm(sin, imag)) * scale
        back_imag = (mm(cos, imag) + mm(sin, real)) * scale
        for side in range(2):
            cut = slice(side * lanes, (side + 1) * lanes)
            k = half * 2 + side
            wide_ref[pl.ds(k, height, stride=step), :] = back_real[:, cut]
            wide_ref[pl.ds(count + k, height, stride=step), :] = back_imag[:, cut]
        return carry

    lax.fori_loop(0, count // 2, body, 0)
    o_ref[...] = wide_ref[...].astype(bf16)


def inverse_kernel(scale, me_ref, x_ref, table_ref, t_ref, gain_ref, *o_refs):
    ways = len(o_refs) // 2
    rows, width, lanes = t_ref.shape
    count = 2 * rows
    tail = table_ref[:, width:].astype(f32)
    flipped = (tail[:, 0:count] + tail[:, count : 2 * count]) + tail[:, 2 * count : 3 * count]
    column = lax.broadcasted_iota(jnp.int32, flipped.shape, 1)
    for shift in range(ways):
        owner = lax.rem(me_ref[0] + shift, ways)
        sides = [
            x_ref[:, 2 * owner + side].astype(f32).reshape(-1, lanes).astype(bf16) for side in range(2)
        ]
        out = mm(table_ref[:, 0:width], jnp.concatenate(sides, axis=1)) * scale
        for side in range(2):
            row = 2 * owner + side
            source = t_ref[row].astype(f32)
            center = jnp.sum(jnp.where(column == row, flipped, 0.0), axis=1, keepdims=True)
            factor = jnp.sum(jnp.where(column == row + rows, flipped, 0.0), axis=1, keepdims=True)
            normed = (source - center) * factor * gain_ref[...]
            o_refs[side * ways + shift][...] = (
                (out[:, side * lanes : (side + 1) * lanes] + normed) + source
            ).astype(bf16)


def gelu(values):
    return 0.5 * values * (1.0 + lax.erf(values * math.sqrt(0.5)))


def eye(rows, columns):
    row = lax.broadcasted_iota(jnp.int32, (rows, columns), 0)
    column = lax.broadcasted_iota(jnp.int32, (rows, columns), 1)
    return jnp.where(row == column, 1.0, 0.0)


def mlp_kernel(
    tile, me_ref, x0, x1, x2, x3, wa_ref, wb_ref, gain_ref, bias_ref, y0, y1, y2, y3, x_ref, y_ref, w_ref, sems
):
    ways, tokens, lanes = x_ref.shape
    channels = ways * lanes
    me = me_ref[0]
    count, hidden_block = w_ref.shape[0], w_ref.shape[1]
    per_side = wa_ref.shape[0] // hidden_block
    fetches = [
        pltpu.make_async_copy(
            (wa_ref, wb_ref)[block // per_side].at[pl.ds(block % per_side * hidden_block, hidden_block)],
            w_ref.at[block],
            sems.at[block],
        )
        for block in range(count)
    ]
    for fetch in fetches:
        fetch.start()
    for shift, ref in enumerate((x0, x1, x2, x3)):
        x_ref[lax.rem(me + ways - shift, ways)] = ref[...]
    unit = eye(8, lanes).astype(bf16)

    def body(index, carry):
        span = pl.ds(pl.multiple_of(index * tile, tile), tile)
        mixed = [x_ref[block, span, :].astype(f32) for block in range(ways)]
        total = sum(mixed[1:], mixed[0])
        square = sum((m * m for m in mixed[1:]), mixed[0] * mixed[0])
        center = jnp.sum(total, axis=1, keepdims=True) / channels
        spread = jnp.sum(square, axis=1, keepdims=True) / channels - center * center
        inverse = lax.rsqrt(spread + norm_eps)
        normed = jnp.concatenate(
            [
                ((m - center) * inverse * gain_ref[:, b * lanes : (b + 1) * lanes]).astype(bf16)
                for b, m in enumerate(mixed)
            ],
            axis=1,
        )
        acc = None
        for block in range(count):
            pl.when(index == 0)(fetches[block].wait)
            bias = mm_t(unit, w_ref[block, :, 2 * channels :])[0:1]
            hidden = gelu(mm_t(normed, w_ref[block, :, :channels]) + bias).astype(bf16)
            product = mm(hidden, w_ref[block, :, channels : 2 * channels])
            acc = product if acc is None else acc + product
        for b in range(ways):
            cut = slice(b * lanes, (b + 1) * lanes)
            y_ref[b, span, :] = (mixed[b] + acc[:, cut] + bias_ref[b : b + 1, :]).astype(bf16)
        return carry

    lax.fori_loop(0, tokens // tile, body, 0)
    for shift, ref in enumerate((y0, y1, y2, y3)):
        ref[...] = y_ref[lax.rem(me + shift, ways)]


def place_kernel(me_ref, *refs):
    *parts, o_ref = refs
    ways = o_ref.shape[0]
    half = o_ref.shape[1] // 2
    for place, part in enumerate(parts):
        shift = place % ways
        o_ref[lax.rem(me_ref[0] + ways - shift, ways), pl.ds(place // ways * half, half), :] = part[...]


def piece_kernel(piece_ref, one_ref, bias_ref, two_ref, out_ref, o_ref, flat_ref):
    channels = one_ref.shape[0]
    lanes = o_ref.shape[1] - 2 * channels
    units = o_ref.shape[0] // 2
    square = eye(lanes, lanes)
    place = lax.broadcasted_iota(jnp.int32, (units, lanes), 1)
    extra = jnp.sum(square * out_ref[...].astype(f32), axis=1, keepdims=True)
    for half in range(2):
        first = half * (one_ref.shape[1] // 2) + piece_ref[half] * units
        slab = pl.ds(pl.multiple_of(first // lanes * lanes, lanes), lanes)
        flat_ref[:, 0:channels] = mm_t(square.astype(bf16), one_ref[:, slab])
        flat_ref[:, channels:] = square * bias_ref[:, slab].astype(f32)
        within = pl.ds(pl.multiple_of(lax.rem(first, lanes), units), units)
        target = pl.ds(half * units, units)
        o_ref[target, 0:channels] = flat_ref[within, 0:channels].astype(bf16)
        o_ref[target, channels : 2 * channels] = two_ref[pl.ds(pl.multiple_of(first, units), units), :]
        bias = jnp.sum(flat_ref[within, channels:], axis=1, keepdims=True)
        near = extra[half * units : (half + 1) * units]
        far = extra[(2 + half) * units : (3 + half) * units]
        values = jnp.where(place == 0, bias, jnp.where(place == 1, near, jnp.where(place == 2, far, 0.0)))
        o_ref[target, 2 * channels :] = values.astype(bf16)


def split_kernel(me_ref, *refs):
    *parts, first_ref, second_ref, bias_ref = refs
    ways = len(parts)
    lanes = bias_ref.shape[1]
    size = first_ref.shape[0] // ways
    for place, part in enumerate(parts):
        for half, ref in enumerate((first_ref, second_ref)):
            ref[place * size : (place + 1) * size, :] = part[half * size : (half + 1) * size, :]
        found = mm_t(eye(8, lanes).astype(bf16), part[:, part.shape[1] - lanes :])
        row = jnp.concatenate([found[1:2], found[2:3]], axis=1)
        bias_ref[pl.ds(lax.rem(me_ref[0] + ways - place, ways), 1), :] = row


def join_kernel(*refs):
    *parts, o_ref = refs
    start = 0
    for part in parts:
        o_ref[start : start + part.shape[0], :] = part[...]
        start += part.shape[0]


def vmem(count):
    return [pl.BlockSpec(memory_space=pltpu.VMEM)] * count


smem = pl.BlockSpec(memory_space=pltpu.SMEM)


def call(kernel, shapes, in_specs, scratch=(), flops=0, size=0):
    return pl.pallas_call(
        kernel,
        out_shape=shapes,
        in_specs=in_specs,
        out_specs=jax.tree.map(lambda _: pl.BlockSpec(memory_space=pltpu.VMEM), shapes),
        scratch_shapes=scratch,
        cost_estimate=pl.CostEstimate(flops=flops, bytes_accessed=size, transcendentals=0),
        compiler_params=pltpu.CompilerParams(vmem_limit_bytes=24 * 1024 * 1024),
    )


def shape(dims, dtype):
    return jax.ShapeDtypeStruct(dims, dtype)


def shifts(value_of, axis, ways):
    return [
        lax.ppermute(value_of(shift), axis, [(i, (i + shift) % ways) for i in range(ways)])
        for shift in range(1, ways)
    ]


def local(
    tokens,
    gain_in,
    spectral_w1,
    spectral_b1,
    spectral_w2,
    spectral_b2,
    gain_out,
    fc1_weight,
    fc1_bias,
    fc2_weight,
    fc2_bias,
):
    rows, width, lanes = tokens.shape
    ways = lax.axis_size("chan")
    owners = lax.axis_size("rows")
    height = rows * owners
    channels = lanes * ways
    per_owner = width // 2 // owners
    me = lax.axis_index("chan").astype(jnp.int32).reshape(1)
    turns = jnp.asarray(circle_table(height), bf16)
    half_scale = 2.0 ** math.floor(math.log2(math.sqrt(width)))
    first_scale, second_scale = 1.0 / half_scale, half_scale / math.sqrt(width * height)

    stats = call(stats_kernel, shape((2, rows, width), f32), vmem(1))(tokens)
    other = lax.ppermute(stats, "chan", [(i, i ^ 1) for i in range(ways)])
    left = call(add_kernel, shape(stats.shape, f32), vmem(2))(stats, other)
    right = lax.ppermute(left, "chan", [(i, i ^ 2) for i in range(ways)])
    table, gain = call(
        partial(table_kernel, per_owner),
        [shape((width, width), bf16), shape((1, lanes), f32)],
        vmem(2),
        scratch=[pltpu.VMEM((width // 2, lanes), f32), pltpu.VMEM((width, lanes), f32)],
    )(turns, gain_in.reshape(1, lanes))
    spectra = call(
        partial(forward_kernel, channels, first_scale),
        shape((owners, rows, 2 * per_owner, lanes), bf16),
        vmem(5),
    )(tokens, left, right, gain, table)
    columns = lax.all_to_all(spectra, "rows", split_axis=0, concat_axis=0)

    ring_x, ring_y, per_x = 4, 4, owners // 4
    place = lax.axis_index("rows").astype(jnp.int32)
    units = fc1_weight.shape[1] // (2 * ring_x)
    across, along, core = place // per_x, place // 2 % ring_y, place % 2
    piece = jnp.stack([across * 2 + core, along * 2 + core])
    mine = call(
        piece_kernel,
        shape((units, 2 * channels + lanes), bf16),
        [smem] + vmem(4),
        scratch=[pltpu.VMEM((lanes, channels + lanes), f32)],
    )(piece, fc1_weight, fc1_bias.reshape(1, -1), fc2_weight, fc2_bias.reshape(1, lanes))
    circle = call(turn_kernel, shape((2 * height + 2 * lanes + 16, height), bf16), vmem(5))(
        turns, spectral_w1, spectral_b1, spectral_w2, spectral_b2
    )
    stage = [mine] + shifts(lambda s: mine, "chan", ways)
    count = ways * units // 2
    *sides, out_bias = call(
        split_kernel,
        [shape((count, mine.shape[1]), bf16)] * 2 + [shape((8, lanes), f32)],
        [smem] + vmem(ways),
    )(me, *stage)
    parts = list(sides)
    for shift in range(1, ring_x):
        ring = [
            [(i, (i + shift * per_x) % owners) for i in range(owners)],
            [(i, i + 2 * ((i // 2 % ring_y + shift) % ring_y - i // 2 % ring_y)) for i in range(owners)],
        ]
        for half in range(2):
            parts.append(lax.ppermute(sides[half], "rows", ring[half]))

    total = owners * rows * 2 * per_owner
    back = call(
        partial(column_kernel, second_scale),
        shape((total, lanes), bf16),
        vmem(2),
        scratch=[
            pltpu.VMEM((total, lanes), f32),
            pltpu.VMEM((height, per_owner * lanes), bf16),
            pltpu.VMEM((height, per_owner * lanes), bf16),
        ],
    )(columns.reshape(total, lanes), circle)
    returned = lax.all_to_all(
        back.reshape(owners, rows, 2 * per_owner, lanes), "rows", split_axis=0, concat_axis=0
    )
    inverse = call(
        partial(flip_kernel, per_owner, lanes, channels), shape((width, width + lanes), bf16), vmem(3)
    )(table, left, right)
    share = rows // ways * width // 2
    mixed = call(
        partial(inverse_kernel, first_scale),
        [shape((share, lanes), bf16)] * (2 * ways),
        [smem] + vmem(4),
    )(me, returned, inverse, tokens, gain_in.reshape(1, lanes))
    halves = [mixed[:ways], mixed[ways:]]
    whole_a = [halves[0][0]] + shifts(lambda s: halves[0][s], "chan", ways)
    near = call(join_kernel, shape((2 * ring_x * parts[0].shape[0], parts[0].shape[1]), bf16), vmem(len(parts)))(*parts)
    far = lax.ppermute(near, "rows", [(i, i ^ 1) for i in range(owners)])
    whole_b = [halves[1][0]] + shifts(lambda s: halves[1][s], "chan", ways)

    def mlp(whole):
        return call(
            partial(mlp_kernel, 256),
            [shape((share, lanes), bf16)] * ways,
            [smem] + vmem(4) + [pl.BlockSpec(memory_space=pl.ANY)] * 2 + vmem(2),
            scratch=[
                pltpu.VMEM((ways, share, lanes), bf16),
                pltpu.VMEM((ways, share, lanes), bf16),
                pltpu.VMEM((4, near.shape[0] // 2, near.shape[1]), bf16),
                pltpu.SemaphoreType.DMA((4,)),
            ],
        )(me, *whole, near, far, gain_out.reshape(1, channels), out_bias)

    result_a = mlp(whole_a)
    parts_a = [result_a[0]] + shifts(lambda s: result_a[s], "chan", ways)
    result_b = mlp(whole_b)
    parts_b = [result_b[0]] + shifts(lambda s: result_b[s], "chan", ways)
    final = call(place_kernel, shape((ways, 2 * share, lanes), bf16), [smem] + vmem(2 * ways))(
        me, *parts_a, *parts_b
    )
    return final.reshape(rows, width, lanes)


def solution(mesh):
    return jax.shard_map(
        local,
        mesh=mesh,
        in_specs=(
            P("rows", None, "chan"),
            P("chan"),
            P(None, "chan", None, None),
            P(None, "chan", None),
            P(None, "chan", None, None),
            P(None, "chan", None),
            P(),
            P(None, "chan"),
            P("chan"),
            P("chan", None),
            P("chan"),
        ),
        out_specs=P("rows", None, "chan"),
        check_vma=False,
    )
```

```python
import math
from functools import partial

import jax
import jax.numpy as jnp
import numpy as np
from jax import lax
from jax.experimental import pallas as pl
from jax.experimental.pallas import tpu as pltpu
from jax.sharding import PartitionSpec as P

norm_eps = 1e-05
shrink_level = 0.01
bf16 = jnp.bfloat16
f32 = jnp.float32


def circle_table(size):
    grid = np.arange(size)
    turn = 2.0 * np.pi / size * ((grid[:, None] * grid[None, :]) % size)
    return np.concatenate([np.cos(turn[: size // 2]), np.sin(turn[: size // 2])], axis=0)


def forward_table(width, per_owner):
    owners = width // 2 // per_owner
    place = np.arange(width)
    freq = np.arange(width // 2).reshape(owners, 1, per_owner)
    freq = np.broadcast_to(freq, (owners, 2, per_owner)).reshape(-1)
    part = np.broadcast_to(np.arange(2).reshape(1, 2, 1), (owners, 2, per_owner)).reshape(-1)
    angle = 2.0 * np.pi / width * ((freq[:, None] * place[None, :]) % width)
    return np.where(part[:, None] == 0, np.cos(angle), -np.sin(angle))


def mm(left, right):
    return jnp.dot(left, right, preferred_element_type=f32)


def mm_t(left, right):
    return lax.dot_general(left, right, (((1,), (1,)), ((), ())), preferred_element_type=f32)


def stats_kernel(x_ref, o_ref):
    rows, _, lanes = x_ref.shape
    ones = jnp.ones((8, lanes), bf16)

    for row in range(rows):
        x = x_ref[row]
        wide = x.astype(f32)
        square = wide * wide
        high = square.astype(bf16)
        low = (square - high.astype(f32)).astype(bf16)
        o_ref[0, row : row + 1, :] = mm_t(ones, x)[0:1]
        o_ref[1, row : row + 1, :] = (mm_t(ones, high) + mm_t(ones, low))[0:1]


def add_kernel(left_ref, right_ref, o_ref):
    o_ref[...] = left_ref[...] + right_ref[...]


def warm_kernel(*refs):
    count = len(refs) // 2
    for source, target in zip(refs[:count], refs[count:]):
        target[...] = source[...]


def flip_kernel(per_owner, lanes, table_ref, i_ref):
    for start in range(0, table_ref.shape[0], lanes):
        place = lax.broadcasted_iota(jnp.int32, (lanes, 1), 0) + start
        weight = jnp.where((place == 0) | (place == per_owner), 1.0, 2.0)
        part = table_ref[start : start + lanes, :].astype(f32) * weight
        i_ref[:, start : start + lanes] = jnp.transpose(part).astype(bf16)


def turn_kernel(half_ref, o_ref):
    size, width = half_ref.shape[0] // 2, half_ref.shape[1]
    column = lax.broadcasted_iota(jnp.int32, (size, width), 1)
    sign = jnp.where(column % 2 == 0, 1.0, -1.0)
    for part in range(2):
        top = half_ref[part * size : (part + 1) * size, :]
        o_ref[2 * part * size : (2 * part + 1) * size, :] = top
        o_ref[(2 * part + 1) * size : (2 * part + 2) * size, :] = (top.astype(f32) * sign).astype(bf16)


def moments(left_ref, right_ref, channels):
    center = (left_ref[0] + right_ref[0]) / channels
    spread = (left_ref[1] + right_ref[1]) / channels - center * center
    return jnp.transpose(jnp.concatenate([center, lax.rsqrt(spread + norm_eps)], axis=0))


def normed_row(source, flipped, row, rows, gain):
    return (source - flipped[:, row : row + 1]) * flipped[:, rows + row : rows + row + 1] * gain


def forward_kernel(channels, scale, x_ref, left_ref, right_ref, gain_ref, table_ref, o_ref):
    rows, _, lanes = x_ref.shape
    owners = o_ref.shape[0]
    flipped = moments(left_ref, right_ref, channels)
    gain = gain_ref[...]
    for pair in range(rows // 2):
        sides = [
            normed_row(x_ref[row].astype(f32), flipped, row, rows, gain).astype(bf16)
            for row in (2 * pair, 2 * pair + 1)
        ]
        out = mm(table_ref[...], jnp.concatenate(sides, axis=1)) * scale
        for side in range(2):
            o_ref[:, 2 * pair + side] = (
                out[:, side * lanes : (side + 1) * lanes].reshape(owners, -1, lanes).astype(bf16)
            )


def residual_kernel(channels, x_ref, left_ref, right_ref, gain_ref, o_ref, f_ref):
    rows = x_ref.shape[0]
    f_ref[...] = moments(left_ref, right_ref, channels)
    column = lax.broadcasted_iota(jnp.int32, f_ref.shape, 1)

    def body(row, carry):
        source = x_ref[row].astype(f32)
        center = jnp.sum(jnp.where(column == row, f_ref[...], 0.0), axis=1, keepdims=True)
        factor = jnp.sum(jnp.where(column == row + rows, f_ref[...], 0.0), axis=1, keepdims=True)
        o_ref[row] = (source - center) * factor * gain_ref[...] + source
        return carry

    lax.fori_loop(0, rows, body, 0)


def soften(values):
    return jnp.where(
        values > shrink_level,
        values - shrink_level,
        jnp.where(values < -shrink_level, values + shrink_level, 0.0),
    )


def block_matrix(w_ref, part):
    count, size = w_ref.shape[1], w_ref.shape[2]
    rows = []
    for block in range(count):
        cells = [jnp.zeros((size, size), f32)] * count
        cells[block] = w_ref[part, block]
        rows.append(jnp.concatenate(cells, axis=1))
    return jnp.concatenate(rows, axis=0)


def complex_matrix(w_ref):
    real, imag = block_matrix(w_ref, 0), block_matrix(w_ref, 1)
    return jnp.concatenate(
        [jnp.concatenate([real, imag], axis=1), jnp.concatenate([-imag, real], axis=1)], axis=0
    ).astype(bf16)


def bias_row(b_ref):
    parts, count = b_ref.shape[0], b_ref.shape[1]
    return jnp.concatenate(
        [b_ref[part, block : block + 1, :] for part in range(parts) for block in range(count)], axis=1
    )


def column_kernel(
    scale, x_ref, table_ref, w_ref, o_ref, wide_ref, real_ref, imag_ref
):
    size = w_ref.shape[1]
    tail = w_ref[2 * size :, :].astype(f32)
    bias_one, bias_two = tail[0:1] + tail[1:2], tail[2:3] + tail[3:4]
    height = table_ref.shape[1]
    lanes = x_ref.shape[1]
    step = x_ref.shape[0] // height
    count = step // 2
    wide_ref[...] = x_ref[...].astype(f32)
    for part, target in ((0, real_ref), (1, imag_ref)):
        for k in range(count):
            target[:, k * lanes : (k + 1) * lanes] = wide_ref[
                pl.ds(part * count + k, height, stride=step), :
            ].astype(bf16)

    for half in range(count // 2):
        span = pl.ds(half * 2 * lanes, 2 * lanes)
        cos, sin = table_ref[0:height, :], table_ref[height:, :]
        real, imag = real_ref[:, span], imag_ref[:, span]
        out_real = (mm(cos, real) + mm(sin, imag)) * scale
        out_imag = (mm(cos, imag) - mm(sin, real)) * scale
        next_real, next_imag = [], []
        for side in range(2):
            cut = slice(side * lanes, (side + 1) * lanes)
            both = jnp.concatenate([out_real[:, cut].astype(bf16), out_imag[:, cut].astype(bf16)], axis=1)
            first = jnp.maximum(mm(both, w_ref[0:size, :]) + bias_one, 0.0).astype(bf16)
            second = soften(mm(first, w_ref[size : 2 * size, :]) + bias_two).astype(bf16)
            next_real.append(second[:, :lanes])
            next_imag.append(second[:, lanes:])
        real, imag = jnp.concatenate(next_real, axis=1), jnp.concatenate(next_imag, axis=1)
        back_real = (mm(cos, real) - mm(sin, imag)) * scale
        back_imag = (mm(cos, imag) + mm(sin, real)) * scale
        for side in range(2):
            cut = slice(side * lanes, (side + 1) * lanes)
            k = half * 2 + side
            wide_ref[pl.ds(k, height, stride=step), :] = back_real[:, cut]
            wide_ref[pl.ds(count + k, height, stride=step), :] = back_imag[:, cut]
    o_ref[...] = wide_ref[...].astype(bf16)


def inverse_kernel(scale, me_ref, x_ref, table_ref, r_ref, *o_refs):
    ways = len(o_refs) // 2
    _, _, lanes = r_ref.shape
    for shift in range(ways):
        owner = lax.rem(me_ref[0] + shift, ways)
        sides = [
            x_ref[:, 2 * owner + side].astype(f32).reshape(-1, lanes).astype(bf16) for side in range(2)
        ]
        out = mm(table_ref[...], jnp.concatenate(sides, axis=1)) * scale
        for side in range(2):
            o_refs[side * ways + shift][...] = (
                out[:, side * lanes : (side + 1) * lanes] + r_ref[2 * owner + side]
            ).astype(bf16)


def gelu(values):
    return 0.5 * values * (1.0 + lax.erf(values * math.sqrt(0.5)))


def eye(rows, columns):
    row = lax.broadcasted_iota(jnp.int32, (rows, columns), 0)
    column = lax.broadcasted_iota(jnp.int32, (rows, columns), 1)
    return jnp.where(row == column, 1.0, 0.0)


def mlp_kernel(
    tile, me_ref, x0, x1, x2, x3, wa_ref, wb_ref, gain_ref, bias_ref, y0, y1, y2, y3, x_ref, y_ref
):
    ways, tokens, lanes = x_ref.shape
    channels = ways * lanes
    me = me_ref[0]
    for shift, ref in enumerate((x0, x1, x2, x3)):
        x_ref[lax.rem(me + ways - shift, ways)] = ref[...]
    unit = eye(8, lanes).astype(bf16)
    hidden_block = 512
    blocks = [
        (ref, pl.ds(start, hidden_block))
        for ref in (wa_ref, wb_ref)
        for start in range(0, ref.shape[0], hidden_block)
    ]
    biases = [mm_t(unit, ref[span, 2 * channels :])[0:1] for ref, span in blocks]

    def body(index, carry):
        span = pl.ds(pl.multiple_of(index * tile, tile), tile)
        mixed = [x_ref[block, span, :].astype(f32) for block in range(ways)]
        total = sum(mixed[1:], mixed[0])
        square = sum((m * m for m in mixed[1:]), mixed[0] * mixed[0])
        center = jnp.sum(total, axis=1, keepdims=True) / channels
        spread = jnp.sum(square, axis=1, keepdims=True) / channels - center * center
        inverse = lax.rsqrt(spread + norm_eps)
        normed = jnp.concatenate(
            [
                ((m - center) * inverse * gain_ref[:, b * lanes : (b + 1) * lanes]).astype(bf16)
                for b, m in enumerate(mixed)
            ],
            axis=1,
        )
        acc = None
        for (ref, rows), bias in zip(blocks, biases):
            hidden = gelu(mm_t(normed, ref[rows, :channels]) + bias).astype(bf16)
            product = mm(hidden, ref[rows, channels : 2 * channels])
            acc = product if acc is None else acc + product
        for b in range(ways):
            cut = slice(b * lanes, (b + 1) * lanes)
            y_ref[b, span, :] = (mixed[b] + acc[:, cut] + bias_ref[b : b + 1, :]).astype(bf16)
        return carry

    lax.fori_loop(0, tokens // tile, body, 0)
    for shift, ref in enumerate((y0, y1, y2, y3)):
        ref[...] = y_ref[lax.rem(me + shift, ways)]


def place_kernel(me_ref, *refs):
    *parts, o_ref = refs
    ways = o_ref.shape[0]
    half = o_ref.shape[1] // 2
    for place, part in enumerate(parts):
        shift = place % ways
        o_ref[lax.rem(me_ref[0] + ways - shift, ways), pl.ds(place // ways * half, half), :] = part[...]


def piece_kernel(piece_ref, one_ref, bias_ref, two_ref, out_ref, o_ref, flat_ref):
    channels = one_ref.shape[0]
    lanes = o_ref.shape[1] - 2 * channels
    units = o_ref.shape[0] // 2
    square = eye(lanes, lanes)
    place = lax.broadcasted_iota(jnp.int32, (units, lanes), 1)
    extra = jnp.sum(square * out_ref[...].astype(f32), axis=1, keepdims=True)
    for half in range(2):
        first = half * (one_ref.shape[1] // 2) + piece_ref[half] * units
        slab = pl.ds(pl.multiple_of(first // lanes * lanes, lanes), lanes)
        flat_ref[:, 0:channels] = mm_t(square.astype(bf16), one_ref[:, slab])
        flat_ref[:, channels:] = square * bias_ref[:, slab].astype(f32)
        within = pl.ds(pl.multiple_of(lax.rem(first, lanes), units), units)
        target = pl.ds(half * units, units)
        o_ref[target, 0:channels] = flat_ref[within, 0:channels].astype(bf16)
        o_ref[target, channels : 2 * channels] = two_ref[pl.ds(pl.multiple_of(first, units), units), :]
        bias = jnp.sum(flat_ref[within, channels:], axis=1, keepdims=True)
        near = extra[half * units : (half + 1) * units]
        far = extra[(2 + half) * units : (3 + half) * units]
        values = jnp.where(place == 0, bias, jnp.where(place == 1, near, jnp.where(place == 2, far, 0.0)))
        o_ref[target, 2 * channels :] = values.astype(bf16)


def prep_kernel(w1_ref, b1_ref, w2_ref, b2_ref, o_ref):
    size = o_ref.shape[1]
    o_ref[0:size, :] = complex_matrix(w1_ref)
    o_ref[size : 2 * size, :] = complex_matrix(w2_ref)
    rows = []
    for ref in (b1_ref, b2_ref):
        bias = bias_row(ref)
        high = bias.astype(bf16).astype(f32)
        rows += [high, bias - high]
    rows.append(jnp.zeros((12, size), f32))
    o_ref[2 * size :, :] = jnp.concatenate(rows, axis=0).astype(bf16)


def split_kernel(me_ref, *refs):
    *parts, first_ref, second_ref, bias_ref = refs
    ways = len(parts)
    lanes = bias_ref.shape[1]
    size = first_ref.shape[0] // ways
    for place, part in enumerate(parts):
        for half, ref in enumerate((first_ref, second_ref)):
            ref[place * size : (place + 1) * size, :] = part[half * size : (half + 1) * size, :]
        found = mm_t(eye(8, lanes).astype(bf16), part[:, part.shape[1] - lanes :])
        row = jnp.concatenate([found[1:2], found[2:3]], axis=1)
        bias_ref[pl.ds(lax.rem(me_ref[0] + ways - place, ways), 1), :] = row


def join_kernel(*refs):
    *parts, after_ref, o_ref = refs
    start = 0
    for part in parts:
        o_ref[start : start + part.shape[0], :] = part[...]
        start += part.shape[0]


def vmem(count):
    return [pl.BlockSpec(memory_space=pltpu.VMEM)] * count


smem = pl.BlockSpec(memory_space=pltpu.SMEM)


def call(kernel, shapes, in_specs, scratch=(), flops=0, size=0):
    return pl.pallas_call(
        kernel,
        out_shape=shapes,
        in_specs=in_specs,
        out_specs=jax.tree.map(lambda _: pl.BlockSpec(memory_space=pltpu.VMEM), shapes),
        scratch_shapes=scratch,
        cost_estimate=pl.CostEstimate(flops=flops, bytes_accessed=size, transcendentals=0),
        compiler_params=pltpu.CompilerParams(vmem_limit_bytes=24 * 1024 * 1024),
    )


def shape(dims, dtype):
    return jax.ShapeDtypeStruct(dims, dtype)


def shifts(value_of, axis, ways):
    return [
        lax.ppermute(value_of(shift), axis, [(i, (i + shift) % ways) for i in range(ways)])
        for shift in range(1, ways)
    ]


def local(
    tokens,
    gain_in,
    spectral_w1,
    spectral_b1,
    spectral_w2,
    spectral_b2,
    gain_out,
    fc1_weight,
    fc1_bias,
    fc2_weight,
    fc2_bias,
):
    rows, width, lanes = tokens.shape
    ways = lax.axis_size("chan")
    owners = lax.axis_size("rows")
    height = rows * owners
    channels = lanes * ways
    per_owner = width // 2 // owners
    me = lax.axis_index("chan").astype(jnp.int32).reshape(1)
    forward = jnp.asarray(forward_table(width, per_owner), bf16)
    turns = jnp.asarray(circle_table(height), bf16)
    half_scale = 2.0 ** math.floor(math.log2(math.sqrt(width)))
    first_scale, second_scale = 1.0 / half_scale, half_scale / math.sqrt(width * height)

    stats = call(stats_kernel, shape((2, rows, width), f32), vmem(1))(tokens)
    other = lax.ppermute(stats, "chan", [(i, i ^ 1) for i in range(ways)])
    left = call(add_kernel, shape(stats.shape, f32), vmem(2))(stats, other)
    right = lax.ppermute(left, "chan", [(i, i ^ 2) for i in range(ways)])
    table, gain = call(
        warm_kernel, [shape(forward.shape, bf16), shape((1, lanes), f32)], vmem(2)
    )(forward, gain_in.reshape(1, lanes))
    spectra = call(
        partial(forward_kernel, channels, first_scale),
        shape((owners, rows, 2 * per_owner, lanes), bf16),
        vmem(5),
    )(tokens, left, right, gain, table)
    columns = lax.all_to_all(spectra, "rows", split_axis=0, concat_axis=0)

    ring_x, ring_y, per_x = 4, 4, owners // 4
    place = lax.axis_index("rows").astype(jnp.int32)
    units = fc1_weight.shape[1] // (2 * ring_x)
    across, along, core = place // per_x, place // 2 % ring_y, place % 2
    piece = jnp.stack([across * 2 + core, along * 2 + core])
    mine = call(
        piece_kernel,
        shape((units, 2 * channels + lanes), bf16),
        [smem] + vmem(4),
        scratch=[pltpu.VMEM((lanes, channels + lanes), f32)],
    )(piece, fc1_weight, fc1_bias.reshape(1, -1), fc2_weight, fc2_bias.reshape(1, lanes))
    wide = 2 * lanes
    spectral = call(prep_kernel, shape((2 * wide + 16, wide), bf16), vmem(4))(
        spectral_w1, spectral_b1, spectral_w2, spectral_b2
    )
    circle = call(turn_kernel, shape((2 * height, height), bf16), vmem(1))(turns)
    stage = [mine] + shifts(lambda s: mine, "chan", ways)
    count = ways * units // 2
    *sides, out_bias = call(
        split_kernel,
        [shape((count, mine.shape[1]), bf16)] * 2 + [shape((8, lanes), f32)],
        [smem] + vmem(ways),
    )(me, *stage)
    parts = list(sides)
    for shift in range(1, ring_x):
        ring = [
            [(i, (i + shift * per_x) % owners) for i in range(owners)],
            [(i, i + 2 * ((i // 2 % ring_y + shift) % ring_y - i // 2 % ring_y)) for i in range(owners)],
        ]
        for half in range(2):
            parts.append(lax.ppermute(sides[half], "rows", ring[half]))

    total = owners * rows * 2 * per_owner
    back = call(
        partial(column_kernel, second_scale),
        shape((total, lanes), bf16),
        vmem(3),
        scratch=[
            pltpu.VMEM((total, lanes), f32),
            pltpu.VMEM((height, per_owner * lanes), bf16),
            pltpu.VMEM((height, per_owner * lanes), bf16),
        ],
    )(columns.reshape(total, lanes), circle, spectral)
    returned = lax.all_to_all(
        back.reshape(owners, rows, 2 * per_owner, lanes), "rows", split_axis=0, concat_axis=0
    )
    resid = call(
        partial(residual_kernel, channels),
        shape((rows, width, lanes), f32),
        vmem(4),
        scratch=[pltpu.VMEM((width, 2 * rows), f32)],
    )(tokens, left, right, gain_in.reshape(1, lanes))
    inverse = call(partial(flip_kernel, per_owner, lanes), shape((width, width), bf16), vmem(1))(forward)
    share = rows // ways * width // 2
    mixed = call(
        partial(inverse_kernel, first_scale),
        [shape((share, lanes), bf16)] * (2 * ways),
        [smem] + vmem(3),
    )(me, returned, inverse, resid)
    halves = [mixed[:ways], mixed[ways:]]
    whole_a = [halves[0][0]] + shifts(lambda s: halves[0][s], "chan", ways)
    near = call(
        join_kernel,
        shape((2 * ring_x * parts[0].shape[0], parts[0].shape[1]), bf16),
        vmem(len(parts)) + [pl.BlockSpec(memory_space=pl.ANY)],
    )(*parts, mixed[0])
    far = lax.ppermute(near, "rows", [(i, i ^ 1) for i in range(owners)])
    whole_b = [halves[1][0]]
    for shift in range(1, ways):
        whole_b.append(lax.ppermute(halves[1][shift], "chan", [(i, (i + shift) % ways) for i in range(ways)]))

    def mlp(whole):
        return call(
            partial(mlp_kernel, 256),
            [shape((share, lanes), bf16)] * ways,
            [smem] + vmem(8),
            scratch=[
                pltpu.VMEM((ways, share, lanes), bf16),
                pltpu.VMEM((ways, share, lanes), bf16),
            ],
        )(me, *whole, near, far, gain_out.reshape(1, channels), out_bias)

    result_a = mlp(whole_a)
    parts_a = [result_a[0]] + shifts(lambda s: result_a[s], "chan", ways)
    result_b = mlp(whole_b)
    parts_b = [result_b[0]] + shifts(lambda s: result_b[s], "chan", ways)
    final = call(place_kernel, shape((ways, 2 * share, lanes), bf16), [smem] + vmem(2 * ways))(
        me, *parts_a, *parts_b
    )
    return final.reshape(rows, width, lanes)


def solution(mesh):
    return jax.shard_map(
        local,
        mesh=mesh,
        in_specs=(
            P("rows", None, "chan"),
            P("chan"),
            P(None, "chan", None, None),
            P(None, "chan", None),
            P(None, "chan", None, None),
            P(None, "chan", None),
            P(),
            P(None, "chan"),
            P("chan"),
            P("chan", None),
            P("chan"),
        ),
        out_specs=P("rows", None, "chan"),
        check_vma=False,
    )
```
